256 devices in a mesh: row: 8 (over y, x_hi), col: 32 (over x_lo, z, core).
Axes of the slice: x: 4 (x_hi: 2, x_lo: 2; x = x_hi * 2 + x_lo), y: 4, z: 8, core: 2. Of those that a mesh axis runs over, the one named last changes fastest.
Arguments:
- inverse_block: float32 [12288, 12288], P('row', 'col'), may hold values from -6 to 6
- factor_panel: float32 [3, 12288, 256], P(None, ('row', 'col')), may hold values from -0.0546875 to 0.0546875
- diag_inverse: float32 [3, 256, 256], P(None, 'row'), may hold values from -6 to 6
- block_lists: int32 [3, 48], replicated, may hold values from 0 to 47, as said below
- list_counts: int32 [3], replicated, may hold values from 6 to 48, as said below
Outputs:
- solved: float32 [3, 12288, 256], P(None, ('row', 'col'))
- diag_block: float32 [3, 256, 256], P(None, 'row')
The draws below stay inside these ranges and needn't reach their ends.
Inputs may be any that keep to these rules, and one draw needn't show every extreme that they name: `block_lists`: row k is an ordering of all 48 ancestor blocks; its first list_counts[k] entries are the blocks listed for supernode k. `list_counts`: one supernode lists all 48 blocks and one lists 48 // 8 of them.
All inputs are finite; a program needn't handle non-finite values.
Results may differ from the reference program's by a relative error of at most 0.000071.
Values sent between devices are 32-bit elements; how exact they have to be, the bound alone decides.
No kernel may reach another device: no remote copies, remote signals or barrier semaphores. Data moves between devices by JAX's collectives and lax.ppermute only.
A program may use at most 64 MiB of HBM per device.

```python
import jax
import jax.numpy as jnp
from jax import lax

NA = 12288
W = 256
BLK = 256
NSN = 3
NB = 48


def listed_draw(key):
    keys = jax.random.split(jax.random.fold_in(key, 7), 5)
    orders = jnp.stack([jax.random.permutation(keys[0], NB), jax.random.permutation(keys[1], NB), jax.random.permutation(keys[2], NB)]).astype(jnp.int32)
    middle = jax.random.randint(keys[3], (), NB // 8, NB + 1).astype(jnp.int32)
    counts = jnp.stack([jnp.int32(NB), jnp.int32(NB // 8), middle])
    shuffle = jax.random.permutation(keys[4], 3)
    return (orders, counts[shuffle].astype(jnp.int32))


def draw_block_lists(key, part):
    return listed_draw(key)[0]


def draw_list_counts(key, part):
    return listed_draw(key)[1]


def spiked(values, rng, source, target, shards_of, factor):
    owner, partner = [(jnp.arange(values.shape[dim]) // (values.shape[dim] // shards_of)).reshape([-1 if axis == dim else 1 for axis in range(values.ndim)]) for dim in (source, target)]
    chosen = jax.random.permutation(rng, shards_of)[partner]
    strong = (owner == chosen) | (owner == (partner + shards_of // 2) % shards_of)
    return jnp.where(strong, factor * values, values)


def level_of(own_key, dims, cuts, least, high):
    level, own = 1.0, jax.random.fold_in(own_key, 6)
    for position, blocks in cuts:
        heights = jnp.exp(jax.random.uniform(jax.random.fold_in(own, position), (blocks,), jnp.float32, least / len(cuts), high / len(cuts)))
        level = level * jnp.repeat(heights, dims[position] // blocks).reshape([-1 if axis == position else 1 for axis in range(len(dims))])
    return level


def gaussian(rng, extent, deviation, limit, pieces=(), kind=jnp.bfloat16):
    values = jax.random.normal(rng, extent, jnp.float32) * deviation
    if len(pieces) > 0:
        values = level_of(rng, extent, pieces, -0.22, 0.18) * values
    return jnp.clip(values, min=-limit, max=limit).astype(kind)


def noise_with(rng, dims, spread, limit, cuts, heavy, kind=jnp.bfloat16):
    values = spread * jax.random.normal(rng, dims, jnp.float32)
    if cuts:
        values = values * level_of(rng, dims, cuts, -0.22, 0.18)
    return jnp.clip(spiked(values, jax.random.fold_in(rng, 3), *heavy), -limit, limit).astype(kind)


def setup_inputs(seed: int = 0) -> dict:
    streams_of = jax.random.split(jax.random.key(seed), 6)
    inverse_block = noise_with(streams_of[0], (NA, NA), 1.0, 6.0, ((0, 8), (1, 32)), (1, 0, 32, 2.75), jnp.float32)
    factor_panel = gaussian(streams_of[1], (NSN, NA, W), NA ** -0.5, 0.0546875, ((1, 256),), jnp.float32)
    diag_inverse = gaussian(streams_of[2], (NSN, W, W), 1.0, 6.0, ((1, 8),), jnp.float32)
    block_lists = draw_block_lists(jax.random.fold_in(streams_of[5], 71), 0)
    list_counts = draw_list_counts(jax.random.fold_in(streams_of[5], 71), 0)
    return {"inverse_block": inverse_block, "factor_panel": factor_panel, "diag_inverse": diag_inverse, "block_lists": block_lists, "list_counts": list_counts}


def listed_table(block_lists, list_counts, nblocks):
    entries = jnp.arange(block_lists.shape[1], dtype=jnp.int32)
    active = entries[None, :] < list_counts[:, None]
    hits = (block_lists[:, :, None] == jnp.arange(nblocks, dtype=jnp.int32)[None, None, :]) & active[:, :, None]
    return jnp.any(hits, axis=1).astype(jnp.float32)


def reference(inverse_block, factor_panel, diag_inverse, block_lists, list_counts):
    table = listed_table(block_lists, list_counts, NA // BLK)
    listed = jnp.repeat(table, BLK, axis=1)
    masked = factor_panel * listed[:, :, None]
    product = lax.map(lambda panel_rows: jnp.dot(inverse_block, panel_rows, precision=lax.Precision.HIGHEST), masked)
    solved = -listed[:, :, None] * product
    diag_block = diag_inverse - jnp.einsum("knw,knv->kwv", masked, solved, precision=lax.Precision.HIGHEST)
    return solved, diag_block
```

```python
import jax
import jax.numpy as jnp
import numpy as np
from jax import lax
from jax.sharding import PartitionSpec as P

BLK = 256
NSN = 3
DIMS = (4, 2, 2, 8, 2)
AXES = ("row", "col")
HIGH = lax.Precision.HIGH


def send(array, target):
    pairs = []
    for source in range(int(np.prod(DIMS))):
        place = tuple(int(i) for i in np.unravel_index(source, DIMS))
        pairs.append((source, int(np.ravel_multi_index(target(*place), DIMS))))
    return lax.ppermute(array, AXES, pairs)


def other_core(y, xh, xl, z, c):
    return (y, xh, xl, z, 1 - c)


def other_xl(y, xh, xl, z, c):
    return (y, xh, 1 - xl, z, c)


def other_xh(y, xh, xl, z, c):
    return (y, 1 - xh, xl, z, c)


def y_up(y, xh, xl, z, c):
    return ((y + 1) % 4, xh, xl, z, c)


def y_down(y, xh, xl, z, c):
    return ((y + 3) % 4, xh, xl, z, c)


def y_by_core(y, xh, xl, z, c):
    return ((y + 1 - 2 * c) % 4, xh, xl, z, c)


def z_by_core(y, xh, xl, z, c):
    return (y, xh, xl, (z + 1 - 2 * c) % 8, c)


def y_flip(bit):
    return lambda y, xh, xl, z, c: (y ^ bit, xh, xl, z, c)


def z_flip(bit):
    return lambda y, xh, xl, z, c: (y, xh, xl, z ^ bit, c)


def to_column(y, xh, xl, z, c):
    return ((y + z % 4) % 4, xh ^ c, y >> 1, (y & 1) * 4 + xh * 2 + xl, z >> 2)


def local_mask(block_lists, list_counts, first_row, count):
    blocks = (first_row + jnp.arange(count, dtype=jnp.int32)) // BLK
    entries = jnp.arange(block_lists.shape[1], dtype=jnp.int32)
    active = entries[None, :] < list_counts[:, None]
    hits = (block_lists[:, None, :] == blocks[None, :, None]) & active[:, None, :]
    return jnp.any(hits, axis=2).astype(jnp.float32)


def pick(array, index, axis):
    return lax.dynamic_index_in_dim(array, index, axis, keepdims=False)


def dot(left, right):
    return jnp.dot(left, right, precision=HIGH, preferred_element_type=jnp.float32)


def per_device(inverse_block, factor_panel, diag_inverse, block_lists, list_counts):
    row, col = lax.axis_index("row"), lax.axis_index("col")
    y, xh = row // 2, row % 2
    xl, z, core = col // 16, col // 2 % 8, col % 2
    nsn, rows, width = factor_panel.shape
    span = inverse_block.shape[1]

    halves = inverse_block.reshape(16, 2, rows, span)
    s_own = pick(halves, core, 1).reshape(16 * rows, span)
    s_other = send(pick(halves, 1 - core, 1).reshape(16 * rows, span), other_core)

    mask = local_mask(block_lists, list_counts, (row * 32 + col) * rows, rows)
    masked = factor_panel * mask[:, :, None]
    flat = jnp.concatenate([masked[k] for k in range(nsn)], axis=1)
    flat_other = send(flat, other_core)

    share = send(flat, to_column)
    y_from, xh_from = xl * 2 + z // 4, z // 2 % 2
    near = send(share, other_xh)
    swapped = (xh ^ xh_from) == 1
    pair = jnp.concatenate([jnp.where(swapped, near, share), jnp.where(swapped, share, near)])
    below, above = send(pair, y_up), send(pair, y_down)
    far = send(jnp.where(core == 0, below, above), y_by_core)
    ring = jnp.stack([pair, above, far, below, pair, above, far])
    m_own = lax.dynamic_slice_in_dim(ring, (y_from - y) % 4, 4, 0).reshape(span, nsn * width)
    m_other = send(m_own, other_core)

    product = dot(s_own, m_own) + dot(s_other, m_other)
    product = product.reshape(2, 8, rows, nsn * width)

    step = 1 - 2 * core
    away, home = pick(product, 1 - xl, 0), pick(product, xl, 0)
    sum_away, sum_home = pick(away, (z - step) % 8, 0), pick(home, (z - step) % 8, 0)
    for t in range(7):
        place = (z - step * (2 + t)) % 8
        sum_away = send(sum_away, z_by_core) + pick(away, place, 0)
        sum_home = send(sum_home, z_by_core) + pick(home, place, 0)
    total = sum_home + send(sum_away, other_xl)
    solved = jnp.stack([total[:, k * width : (k + 1) * width] for k in range(nsn)])
    solved = -solved * mask[:, :, None]

    half = width // 2
    columns = solved.reshape(nsn, rows, 2, half)
    x_own = pick(columns, core, 2)
    x_other = send(pick(columns, 1 - core, 2), other_core)
    terms = []
    for k in range(nsn):
        left = jnp.concatenate([flat[:, k * width : (k + 1) * width], flat_other[:, k * width : (k + 1) * width]])
        right = jnp.concatenate([x_own[k], x_other[k]])
        terms.append(
            lax.dot_general(left, right, (((0,), (0,)), ((), ())), precision=HIGH, preferred_element_type=jnp.float32)
        )
    terms = jnp.stack(terms).reshape(nsn, 2, 2, 2, width // 8, half)
    terms = pick(terms, xh, 3) + send(pick(terms, 1 - xh, 3), other_xh)
    terms = pick(terms, y % 2, 2) + send(pick(terms, 1 - y % 2, 2), y_flip(1))
    terms = pick(terms, y // 2, 1) + send(pick(terms, 1 - y // 2, 1), y_flip(2))
    terms = terms + send(terms, other_xl)
    for bit in (1, 2, 4):
        terms = terms + send(terms, z_flip(bit))
    rest = send(terms, other_core)
    first = jnp.where(core == 0, terms, rest)
    second = jnp.where(core == 0, rest, terms)
    diag_block = diag_inverse - jnp.concatenate([first, second], axis=2)
    return (solved, diag_block)


def solution(mesh):
    placed = (P("row", "col"), P(None, ("row", "col"), None), P(None, "row", None), P(), P())
    return jax.shard_map(
        per_device,
        mesh=mesh,
        in_specs=placed,
        out_specs=(P(None, ("row", "col"), None), P(None, "row", None)),
        check_vma=False,
    )
```

```python
import itertools

import jax
import jax.numpy as jnp
import numpy as np
from jax import lax
from jax.experimental import pallas as pl
from jax.experimental.pallas import tpu as pltpu
from jax.sharding import PartitionSpec as P

BLK = 256
DIMS = (4, 2, 2, 8, 2)
AXES = ("row", "col")
HIGH = lax.Precision.HIGH


def send(array, target):
    pairs = []
    for source in range(int(np.prod(DIMS))):
        place = tuple(int(i) for i in np.unravel_index(source, DIMS))
        pairs.append((source, int(np.ravel_multi_index(target(*place), DIMS))))
    return lax.ppermute(array, AXES, pairs)


def other_core(y, xh, xl, z, c):
    return (y, xh, xl, z, 1 - c)


def other_xl(y, xh, xl, z, c):
    return (y, xh, 1 - xl, z, c)


def other_xh(y, xh, xl, z, c):
    return (y, 1 - xh, xl, z, c)


def y_by(move):
    return lambda y, xh, xl, z, c: ((y + move(c)) % 4, xh, xl, z, c)


def z_by(move):
    return lambda y, xh, xl, z, c: (y, xh, xl, (z + move(c)) % 8, c)


def y_pair(y, xh, xl, z, c):
    return (y ^ (3 if c else 1), xh, xl, z, c)


def z_pair(bit):
    return lambda y, xh, xl, z, c: (y, xh, xl, (((z + c) % 8 ^ bit) - c) % 8, c)


def ring_distance(a, b, size):
    return min((a - b) % size, (b - a) % size)


def column_slots():
    target, share_of = {}, np.zeros((2, 8, 4, 2, 2), np.int32)
    for xl, z in itertools.product(range(2), range(8)):
        ys, xhs, xls = xl * 2 + z // 4, z // 2 % 2, z % 2
        shares = sorted(itertools.product(range(8), range(2)), key=lambda s: (-ring_distance(s[0], z, 8), s))
        slots = sorted(
            itertools.product(range(4), range(2), range(2)),
            key=lambda s: (ring_distance(s[0], ys, 4) + 2 * (s[1] != xhs), s),
        )
        for (zs, cs), (y, xh, c) in zip(shares, slots):
            target[(ys, xhs, xls, zs, cs)] = (y, xh, xl, z, c)
            share_of[xl, z, y, xh, c] = zs * 2 + cs
    return target, share_of


COLUMN_TARGET, SHARE_OF = column_slots()


def to_column(*place):
    return COLUMN_TARGET[place]


def listed_blocks(block_lists, list_counts, blocks):
    entries = jnp.arange(block_lists.shape[1], dtype=jnp.int32)
    active = entries[None, :] < list_counts[:, None]
    hits = (block_lists[:, None, :] == blocks[None, :, None]) & active[:, None, :]
    return jnp.any(hits, axis=2)


def pick(array, index, axis):
    return lax.dynamic_index_in_dim(array, index, axis, keepdims=False)


def place_of(row, col):
    return row // 2, row % 2, col // 16, col // 2 % 8, col % 2


def split(value):
    high = lax.reduce_precision(value, 8, 7)
    return high.astype(jnp.bfloat16), (value - high).astype(jnp.bfloat16)


def multiply_kernel(share_ref, listed_ref, s_high, s_low, *refs):
    pieces, (out, raw, m_high, m_low) = refs[:8], refs[8:]
    nsn, rows, width = pieces[0].shape[0] // 2, pieces[0].shape[1], pieces[0].shape[2]
    y, xh, xl, z, core = place_of(lax.axis_index("row"), lax.axis_index("col"))
    column = xl * 8 + z
    for j, piece in enumerate(pieces):
        dy, c = j % 4, (core if j < 4 else 1 - core)
        for dxh in range(2):
            slot = ((y + dy) % 4 * 2 + (xh + dxh) % 2) * 2 + c
            start = pl.multiple_of(share_ref[column * 16 + slot] * rows, 8)
            for k in range(nsn):
                raw[pl.ds(start, rows), k * width : (k + 1) * width] = piece[dxh * nsn + k]
    count = raw.shape[0] // BLK
    for b in range(count):
        for k in range(nsn):
            flag = listed_ref[k, column * count + b].astype(jnp.float32)
            value = raw[b * BLK : (b + 1) * BLK, k * width : (k + 1) * width] * flag
            high = value.astype(jnp.bfloat16)
            m_high[b * BLK : (b + 1) * BLK, k * width : (k + 1) * width] = high
            m_low[b * BLK : (b + 1) * BLK, k * width : (k + 1) * width] = (
                value - high.astype(jnp.float32)
            ).astype(jnp.bfloat16)

    def dot(left, right):
        return jnp.dot(left, right, preferred_element_type=jnp.float32)

    for i in range(out.shape[0] // BLK):
        band = slice(i * BLK, (i + 1) * BLK)
        out[band, :] = (
            dot(s_high[band, :], m_high[...]) + dot(s_high[band, :], m_low[...]) + dot(s_low[band, :], m_high[...])
        )


def multiply(listed, s_high, s_low, pieces):
    size = s_high.shape[0]
    wide = pieces[0].shape[0] // 2 * pieces[0].shape[2]
    depth = s_high.shape[1]
    whole = pl.BlockSpec(memory_space=pltpu.VMEM)
    scalars = pl.BlockSpec(memory_space=pltpu.SMEM)
    return pl.pallas_call(
        multiply_kernel,
        out_shape=jax.ShapeDtypeStruct((size, wide), jnp.float32),
        in_specs=[scalars, scalars] + [whole] * (2 + len(pieces)),
        out_specs=whole,
        scratch_shapes=[
            pltpu.VMEM((depth, wide), jnp.float32),
            pltpu.VMEM((depth, wide), jnp.bfloat16),
            pltpu.VMEM((depth, wide), jnp.bfloat16),
        ],
        cost_estimate=pl.CostEstimate(flops=6 * size * wide * depth, bytes_accessed=12 * size * wide, transcendentals=0),
        name="multiply",
    )(jnp.asarray(SHARE_OF.reshape(-1)), listed, s_high, s_low, *pieces)


def per_device(inverse_block, factor_panel, diag_inverse, block_lists, list_counts):
    row, col = lax.axis_index("row"), lax.axis_index("col")
    y, xh, xl, z, core = place_of(row, col)
    nsn, rows, width = factor_panel.shape
    span = inverse_block.shape[1]
    half = width // 2

    share = send(factor_panel, to_column)
    near = send(share, other_xh)
    pair = jnp.concatenate([share, near])
    below, above = send(pair, y_by(lambda c: 1)), send(pair, y_by(lambda c: -1))
    far = send(jnp.where(core == 0, below, above), y_by(lambda c: 1 - 2 * c))
    pieces = [pair, above, far, below]
    pieces = pieces + [send(piece, other_core) for piece in pieces]

    halves = inverse_block.reshape(16, 2, rows, span)
    s_own = pick(halves, core, 1).reshape(16 * rows, span)
    s_other = send(pick(halves, 1 - core, 1).reshape(16 * rows, span), other_core)
    s_chip = jnp.concatenate(
        [jnp.where(core == 0, s_own, s_other), jnp.where(core == 0, s_other, s_own)], axis=1
    )
    s_high, s_low = split(s_chip)
    listed = listed_blocks(block_lists, list_counts, jnp.arange(block_lists.shape[1], dtype=jnp.int32))
    product = multiply(listed.astype(jnp.int32), s_high, s_low, pieces)
    product = product.reshape(2, 8, rows, nsn * width)

    row_blocks = ((row * 32 + col) * rows + jnp.arange(rows, dtype=jnp.int32)) // BLK
    mask = listed_blocks(block_lists, list_counts, row_blocks).astype(jnp.float32)
    masked = factor_panel * mask[:, :, None]
    masked_xl = send(masked, other_xl)
    left = jnp.concatenate(
        [jnp.where(xl == 0, masked, masked_xl), jnp.where(xl == 0, masked_xl, masked)], axis=1
    )
    left = jnp.concatenate([left, send(left, other_core)], axis=1)

    def at(distance):
        return pick(product, (z + distance) % 8, 1)

    first = send(at(4), z_by(lambda c: 1 - 2 * c))
    up = at(3) + jnp.where(core == 0, first, 0.0)
    down = at(-3) + jnp.where(core == 1, first, 0.0)
    for distance in (2, 1, 0):
        up, down = send(up, z_by(lambda c: 1)), send(down, z_by(lambda c: -1))
        if distance:
            up, down = at(distance) + up, at(-distance) + down
    partial = at(0) + up + down

    total = pick(partial, xl, 0) + send(pick(partial, 1 - xl, 0), other_xl)
    solved = jnp.stack([total[:, k * width : (k + 1) * width] for k in range(nsn)])
    solved = -solved * mask[:, :, None]

    columns = partial.reshape(2 * rows, nsn, 2, half)
    right = pick(columns, core, 2)
    right = jnp.concatenate([right, send(pick(columns, 1 - core, 2), other_core)])
    terms = jnp.stack(
        [
            lax.dot_general(
                left[k], right[:, k], (((0,), (0,)), ((), ())), precision=HIGH, preferred_element_type=jnp.float32
            )
            for k in range(nsn)
        ]
    )
    terms = terms.reshape(nsn, 2, 2, 2, width // 8, half)
    terms = pick(terms, y % 2, 2) + send(pick(terms, 1 - y % 2, 2), y_pair)
    terms = pick(terms, y // 2, 1) + send(pick(terms, 1 - y // 2, 1), y_by(lambda c: 2))
    terms = pick(terms, xh, 1) + send(pick(terms, 1 - xh, 1), other_xh)
    terms = terms + send(terms, other_xl)
    for bit in (1, 2, 4):
        terms = terms + send(terms, z_pair(bit))
    rest = send(terms, other_core)
    diag_block = diag_inverse + jnp.concatenate(
        [jnp.where(core == 0, terms, rest), jnp.where(core == 0, rest, terms)], axis=2
    )
    return (solved, diag_block)


def solution(mesh):
    placed = (P("row", "col"), P(None, ("row", "col"), None), P(None, "row", None), P(), P())
    return jax.shard_map(
        per_device,
        mesh=mesh,
        in_specs=placed,
        out_specs=(P(None, ("row", "col"), None), P(None, "row", None)),
        check_vma=False,
    )
```

```python
import jax
import jax.numpy as jnp
import numpy as np
from jax import lax
from jax.experimental import pallas as pl
from jax.experimental.pallas import tpu as pltpu
from jax.sharding import PartitionSpec as P

BLK = 256
SEGMENT = 16
VMEM_LIMIT = 20 * 1024 * 1024
DIMS = (4, 2, 2, 8, 2)
AXES = ("row", "col")
HIGH = lax.Precision.HIGH


def send(array, target):
    pairs = []
    for source in range(int(np.prod(DIMS))):
        place = tuple(int(i) for i in np.unravel_index(source, DIMS))
        pairs.append((source, int(np.ravel_multi_index(target(*place), DIMS))))
    return lax.ppermute(array, AXES, pairs)


def other_core(y, xh, xl, z, c):
    return (y, xh, xl, z, 1 - c)


def other_xl(y, xh, xl, z, c):
    return (y, xh, 1 - xl, z, c)


def other_xh(y, xh, xl, z, c):
    return (y, 1 - xh, xl, z, c)


def y_by(move):
    return lambda y, xh, xl, z, c: ((y + move(c)) % 4, xh, xl, z, c)


def z_by(move):
    return lambda y, xh, xl, z, c: (y, xh, xl, (z + move(c)) % 8, c)


def y_pair(y, xh, xl, z, c):
    return (y ^ (3 if c else 1), xh, xl, z, c)


def z_pair(bit):
    return lambda y, xh, xl, z, c: (y, xh, xl, (((z + c) % 8 ^ bit) - c) % 8, c)


SHARES = (
    (5, 8, 10, 7, 14, 11, 4, 1, 2, 13, 15, 0, 9, 6, 3, 12),
    (11, 7, 4, 10, 0, 9, 3, 13, 5, 14, 1, 2, 12, 15, 6, 8),
    (1, 8, 11, 0, 7, 4, 12, 10, 6, 3, 9, 14, 2, 5, 15, 13),
    (12, 14, 7, 15, 11, 0, 8, 4, 2, 9, 3, 6, 13, 1, 5, 10),
    (8, 7, 13, 4, 11, 0, 14, 3, 10, 1, 12, 5, 2, 15, 6, 9),
    (1, 4, 14, 9, 3, 13, 2, 12, 5, 0, 8, 11, 6, 7, 15, 10),
    (15, 12, 1, 4, 3, 8, 6, 0, 9, 10, 13, 5, 11, 14, 2, 7),
    (9, 3, 13, 0, 15, 6, 2, 7, 12, 4, 5, 8, 1, 10, 11, 14),
    (14, 1, 12, 5, 2, 6, 13, 11, 8, 4, 9, 3, 15, 0, 10, 7),
    (12, 9, 3, 0, 10, 8, 1, 6, 14, 7, 4, 15, 11, 13, 5, 2),
    (5, 0, 3, 6, 14, 2, 1, 9, 13, 4, 10, 12, 11, 7, 8, 15),
    (8, 5, 13, 0, 2, 11, 7, 15, 12, 1, 4, 10, 3, 6, 14, 9),
    (6, 14, 15, 3, 7, 10, 12, 5, 8, 4, 2, 9, 0, 13, 1, 11),
    (1, 2, 9, 10, 4, 15, 11, 8, 7, 3, 14, 13, 12, 6, 5, 0),
    (9, 11, 3, 6, 13, 8, 10, 15, 2, 14, 7, 1, 0, 5, 4, 12),
    (3, 10, 7, 15, 0, 13, 4, 9, 14, 11, 1, 6, 8, 5, 2, 12),
)


def column_target():
    target = {}
    for column, shares in enumerate(SHARES):
        xl, z = column // 8, column % 8
        for slot, share in enumerate(shares):
            source = (xl * 2 + z // 4, z // 2 % 2, z % 2, share // 2, share % 2)
            target[source] = (slot // 4, slot // 2 % 2, xl, z, slot % 2)
    return target


COLUMN_TARGET = column_target()


def to_column(*place):
    return COLUMN_TARGET[place]


def listed_blocks(block_lists, list_counts, blocks):
    entries = jnp.arange(block_lists.shape[1], dtype=jnp.int32)
    active = entries[None, :] < list_counts[:, None]
    hits = (block_lists[:, None, :] == blocks[None, :, None]) & active[:, None, :]
    return jnp.any(hits, axis=2)


def pick(array, index, axis):
    return lax.dynamic_index_in_dim(array, index, axis, keepdims=False)


def place_of(row, col):
    return row // 2, row % 2, col // 16, col // 2 % 8, col % 2


def split(value):
    high = lax.reduce_precision(value, 8, 7)
    return high.astype(jnp.bfloat16), (value - high).astype(jnp.bfloat16)


def split_value(value):
    high = value.astype(jnp.bfloat16)
    return high, (value - high.astype(jnp.float32)).astype(jnp.bfloat16)


def multiply_kernel(share_ref, listed_ref, left_high, left_low, *refs):
    pieces, (out, right_high, right_low) = refs[:8], refs[8:]
    nsn, rows, width = pieces[0].shape[0] // 2, pieces[0].shape[1], pieces[0].shape[2]
    depth = right_high.shape[0]
    y, xh, xl, z, core = place_of(lax.axis_index("row"), lax.axis_index("col"))
    column = xl * 8 + z
    for j, piece in enumerate(pieces):
        dy, c = j % 4, (core if j < 4 else 1 - core)
        for dxh in range(2):
            slot = ((y + dy) % 4 * 2 + (xh + dxh) % 2) * 2 + c
            start = share_ref[column * 16 + slot] * rows
            for part in range(0, rows, SEGMENT):
                place = pl.multiple_of(start + part, SEGMENT)
                block = column * (depth // BLK) + place // BLK
                for k in range(nsn):
                    flag = listed_ref[k, block].astype(jnp.float32)
                    high, low = split_value(piece[dxh * nsn + k, part : part + SEGMENT] * flag)
                    lanes = slice(k * width, (k + 1) * width)
                    right_high[pl.ds(place, SEGMENT), lanes] = high
                    right_low[pl.ds(place, SEGMENT), lanes] = low

    def dot(left, right):
        return jnp.dot(left, right, preferred_element_type=jnp.float32)

    for i in range(0, out.shape[0], BLK):
        band = slice(i, i + BLK)
        out[band, :] = (
            dot(left_high[band, :], right_high[...])
            + dot(left_high[band, :], right_low[...])
            + dot(left_low[band, :], right_high[...])
        )


def multiply(listed, left_high, left_low, pieces):
    size, depth = left_high.shape
    wide = pieces[0].shape[0] // 2 * pieces[0].shape[2]
    whole = pl.BlockSpec(memory_space=pltpu.VMEM)
    scalars = pl.BlockSpec(memory_space=pltpu.SMEM)
    return pl.pallas_call(
        multiply_kernel,
        out_shape=jax.ShapeDtypeStruct((size, wide), jnp.float32),
        in_specs=[scalars, scalars] + [whole] * (2 + len(pieces)),
        out_specs=whole,
        scratch_shapes=[pltpu.VMEM((depth, wide), jnp.bfloat16)] * 2,
        compiler_params=pltpu.CompilerParams(vmem_limit_bytes=VMEM_LIMIT),
        cost_estimate=pl.CostEstimate(flops=6 * size * wide * depth, bytes_accessed=12 * size * wide, transcendentals=0),
        name="multiply",
    )(jnp.asarray(np.array(SHARES, np.int32).reshape(-1)), listed, left_high, left_low, *pieces)


def terms_kernel(listed_ref, product, *refs):
    parts, (keep, give, left_high, left_low, right_high, right_low) = refs[:8], refs[8:]
    nsn, rows, width = parts[0].shape[0] // 2, parts[0].shape[1], parts[0].shape[2]
    row, col = lax.axis_index("row"), lax.axis_index("col")
    _, _, _, z, core = place_of(row, col)
    for d, part in enumerate(parts):
        chip = (z + d) % 8
        for x in range(2):
            here = slice((d * 2 + x) * rows, (d * 2 + x + 1) * rows)
            value = product[pl.ds(pl.multiple_of((x * 8 + chip) * rows, SEGMENT), rows), :]
            right_high[here, :], right_low[here, :] = split_value(value)
            first = (row * 32 + x * 16 + chip * 2 + core) * rows
            for s in range(0, rows, SEGMENT):
                for k in range(nsn):
                    flag = listed_ref[k, (first + s) // BLK].astype(jnp.float32)
                    high, low = split_value(part[x * nsn + k, s : s + SEGMENT] * flag)
                    spot = (slice(here.start + s, here.start + s + SEGMENT), slice(k * width, (k + 1) * width))
                    left_high[spot], left_low[spot] = high, low

    def dot(left, right, lanes):
        return lax.dot_general(
            left[:, lanes], right[:, lanes], (((0,), (0,)), ((), ())), preferred_element_type=jnp.float32
        )

    for k in range(nsn):
        lanes = slice(k * width, (k + 1) * width)
        value = (
            dot(left_high, right_high, lanes) + dot(left_high, right_low, lanes) + dot(left_low, right_high, lanes)
        )
        below, above = value[:, : width // 2], value[:, width // 2 :]
        keep[k] = jnp.where(core == 0, below, above)
        give[k] = jnp.where(core == 0, above, below)


def diagonal_terms(listed, product, parts):
    size, wide = product.shape
    nsn, width = parts[0].shape[0] // 2, parts[0].shape[2]
    whole = pl.BlockSpec(memory_space=pltpu.VMEM)
    return pl.pallas_call(
        terms_kernel,
        out_shape=[jax.ShapeDtypeStruct((nsn, width, width // 2), jnp.float32)] * 2,
        in_specs=[pl.BlockSpec(memory_space=pltpu.SMEM)] + [whole] * (1 + len(parts)),
        out_specs=[whole, whole],
        scratch_shapes=[pltpu.VMEM((size, wide), jnp.bfloat16)] * 4,
        compiler_params=pltpu.CompilerParams(vmem_limit_bytes=VMEM_LIMIT),
        cost_estimate=pl.CostEstimate(
            flops=6 * size * wide * width, bytes_accessed=8 * size * wide, transcendentals=0
        ),
        name="terms",
    )(listed, product, *parts)


def both(*arrays):
    return lax.optimization_barrier(arrays)


def per_device(inverse_block, factor_panel, diag_inverse, block_lists, list_counts):
    row, col = lax.axis_index("row"), lax.axis_index("col")
    y, xh, xl, z, core = place_of(row, col)
    nsn, rows, width = factor_panel.shape
    span = inverse_block.shape[1]

    def facing(array):
        return send(array, other_core)

    share = send(factor_panel, to_column)
    beside = send(factor_panel, other_xl)
    halves = inverse_block.reshape(16, 2, rows, span)
    s_own = pick(halves, core, 1).reshape(16 * rows, span)
    s_other = facing(pick(halves, 1 - core, 1).reshape(16 * rows, span))
    share, beside, s_other = both(share, beside, s_other)

    near = send(share, other_xh)
    line = jnp.concatenate(
        [jnp.where(xl == 0, factor_panel, beside), jnp.where(xl == 0, beside, factor_panel)]
    )
    line_down, line_up = send(line, z_by(lambda c: 1)), send(line, z_by(lambda c: -1))
    s_chip = jnp.concatenate(
        [jnp.where(core == 0, s_own, s_other), jnp.where(core == 0, s_other, s_own)], axis=1
    )
    s_high, s_low = split(s_chip)
    listed = listed_blocks(block_lists, list_counts, jnp.arange(block_lists.shape[1], dtype=jnp.int32))
    listed = listed.astype(jnp.int32)
    near, line_down, line_up, s_high, s_low, listed = both(near, line_down, line_up, s_high, s_low, listed)

    pair = jnp.concatenate([share, near])
    below, above = send(pair, y_by(lambda c: 1)), send(pair, y_by(lambda c: -1))
    line_down2, line_up2 = send(line_down, z_by(lambda c: 1)), send(line_up, z_by(lambda c: -1))
    pair_facing = facing(pair)
    below, above, line_down2, line_up2, pair_facing = both(below, above, line_down2, line_up2, pair_facing)

    far = send(jnp.where(core == 0, below, above), y_by(lambda c: 1 - 2 * c))
    line_down3, line_up3 = send(line_down2, z_by(lambda c: 1)), send(line_up2, z_by(lambda c: -1))
    below_facing, above_facing = facing(below), facing(above)
    far, line_down3, line_up3, below_facing, above_facing = both(
        far, line_down3, line_up3, below_facing, above_facing
    )
    line_far = send(jnp.where(core == 0, line_down3, line_up3), z_by(lambda c: 1 - 2 * c))
    pieces = [pair, above, far, below, pair_facing, above_facing, facing(far), below_facing]
    product = multiply(listed, s_high, s_low, pieces)
    stacked = product.reshape(2, 8, rows, nsn * width)

    def at(distance):
        return pick(stacked, (z + distance) % 8, 1)

    first = send(at(4), z_by(lambda c: 1 - 2 * c))
    up = at(3) + jnp.where(core == 0, first, 0.0)
    down = at(-3) + jnp.where(core == 1, first, 0.0)
    for distance in (2, 1, 0):
        up, down = send(up, z_by(lambda c: 1)), send(down, z_by(lambda c: -1))
        if distance:
            up, down = at(distance) + up, at(-distance) + down
    partial = at(0) + up + down

    row_blocks = ((row * 32 + col) * rows + jnp.arange(rows, dtype=jnp.int32)) // BLK
    mask = listed_blocks(block_lists, list_counts, row_blocks).astype(jnp.float32)
    total = pick(partial, xl, 0) + send(pick(partial, 1 - xl, 0), other_xl)
    solved = jnp.stack([total[:, k * width : (k + 1) * width] for k in range(nsn)])
    solved = -solved * mask[:, :, None]

    keep, give = diagonal_terms(
        listed, product, [line, line_up, line_up2, line_up3, line_far, line_down3, line_down2, line_down]
    )
    terms = (keep + facing(give)).reshape(nsn, 2, 2, 2, width // 8, width // 2)
    terms = pick(terms, y % 2, 2) + send(pick(terms, 1 - y % 2, 2), y_pair)
    terms = pick(terms, y // 2, 1) + send(pick(terms, 1 - y // 2, 1), y_by(lambda c: 2))
    terms = pick(terms, xh, 1) + send(pick(terms, 1 - xh, 1), other_xh)
    terms = terms + send(terms, other_xl)
    for bit in (1, 2, 4):
        terms = terms + send(terms, z_pair(bit))
    rest = facing(terms)
    diag_block = diag_inverse + jnp.concatenate(
        [jnp.where(core == 0, terms, rest), jnp.where(core == 0, rest, terms)], axis=2
    )
    return (solved, diag_block)


def solution(mesh):
    placed = (P("row", "col"), P(None, ("row", "col"), None), P(None, "row", None), P(), P())
    return jax.shard_map(
        per_device,
        mesh=mesh,
        in_specs=placed,
        out_specs=(P(None, ("row", "col"), None), P(None, "row", None)),
        check_vma=False,
    )
```

```python
import jax
import jax.numpy as jnp
import numpy as np
from jax import lax
from jax.experimental import pallas as pl
from jax.experimental.pallas import tpu as pltpu
from jax.sharding import PartitionSpec as P


BLK = 256
SEGMENT = 16
VMEM_LIMIT = 20 * 1024 * 1024
DIMS = (4, 2, 2, 8, 2)
AXES = ("row", "col")


def send(array, target):
    pairs = []
    for source in range(int(np.prod(DIMS))):
        place = tuple(int(i) for i in np.unravel_index(source, DIMS))
        pairs.append((source, int(np.ravel_multi_index(target(*place), DIMS))))
    return lax.ppermute(array, AXES, pairs)


def other_core(y, xh, xl, z, c):
    return (y, xh, xl, z, 1 - c)


def other_xl(y, xh, xl, z, c):
    return (y, xh, 1 - xl, z, c)


def other_xh(y, xh, xl, z, c):
    return (y, 1 - xh, xl, z, c)


def y_by(move):
    return lambda y, xh, xl, z, c: ((y + move(c)) % 4, xh, xl, z, c)


def z_by(move):
    return lambda y, xh, xl, z, c: (y, xh, xl, (z + move(c)) % 8, c)


def y_pair(y, xh, xl, z, c):
    return (y ^ (3 if c else 1), xh, xl, z, c)


def z_pair(bit):
    return lambda y, xh, xl, z, c: (y, xh, xl, (((z + c) % 8 ^ bit) - c) % 8, c)


SHARES = (
    (5, 8, 10, 7, 14, 11, 4, 1, 2, 13, 15, 0, 9, 6, 3, 12),
    (11, 7, 4, 10, 0, 9, 3, 13, 5, 14, 1, 2, 12, 15, 6, 8),
    (1, 8, 11, 0, 7, 4, 12, 10, 6, 3, 9, 14, 2, 5, 15, 13),
    (12, 14, 7, 15, 11, 0, 8, 4, 2, 9, 3, 6, 13, 1, 5, 10),
    (8, 7, 13, 4, 11, 0, 14, 3, 10, 1, 12, 5, 2, 15, 6, 9),
    (1, 4, 14, 9, 3, 13, 2, 12, 5, 0, 8, 11, 6, 7, 15, 10),
    (15, 12, 1, 4, 3, 8, 6, 0, 9, 10, 13, 5, 11, 14, 2, 7),
    (9, 3, 13, 0, 15, 6, 2, 7, 12, 4, 5, 8, 1, 10, 11, 14),
    (14, 1, 12, 5, 2, 6, 13, 11, 8, 4, 9, 3, 15, 0, 10, 7),
    (12, 9, 3, 0, 10, 8, 1, 6, 14, 7, 4, 15, 11, 13, 5, 2),
    (5, 0, 3, 6, 14, 2, 1, 9, 13, 4, 10, 12, 11, 7, 8, 15),
    (8, 5, 13, 0, 2, 11, 7, 15, 12, 1, 4, 10, 3, 6, 14, 9),
    (6, 14, 15, 3, 7, 10, 12, 5, 8, 4, 2, 9, 0, 13, 1, 11),
    (1, 2, 9, 10, 4, 15, 11, 8, 7, 3, 14, 13, 12, 6, 5, 0),
    (9, 11, 3, 6, 13, 8, 10, 15, 2, 14, 7, 1, 0, 5, 4, 12),
    (3, 10, 7, 15, 0, 13, 4, 9, 14, 11, 1, 6, 8, 5, 2, 12),
)


def column_target():
    target = {}
    for column, shares in enumerate(SHARES):
        xl, z = column // 8, column % 8
        for slot, share in enumerate(shares):
            source = (xl * 2 + z // 4, z // 2 % 2, z % 2, share // 2, share % 2)
            target[source] = (slot // 4, slot // 2 % 2, xl, z, slot % 2)
    return target


COLUMN_TARGET = column_target()


def to_column(*place):
    return COLUMN_TARGET[place]


def listed_blocks(block_lists, list_counts, blocks):
    entries = jnp.arange(block_lists.shape[1], dtype=jnp.int32)
    active = entries[None, :] < list_counts[:, None]
    hits = (block_lists[:, None, :] == blocks[None, :, None]) & active[:, None, :]
    return jnp.any(hits, axis=2)


def pick(array, index, axis):
    return lax.dynamic_index_in_dim(array, index, axis, keepdims=False)


def place_of(row, col):
    return row // 2, row % 2, col // 16, col // 2 % 8, col % 2


def split(value):
    high = lax.reduce_precision(value, 8, 7)
    return high.astype(jnp.bfloat16), (value - high).astype(jnp.bfloat16)


def split_value(value):
    high = value.astype(jnp.bfloat16)
    return high, (value - high.astype(jnp.float32)).astype(jnp.bfloat16)


def multiply_kernel(share_ref, listed_ref, left_high, left_low, *refs):
    pieces, (out, opposite, right_high, right_low) = refs[:8], refs[8:]
    nsn, rows, width = pieces[0].shape[0] // 2, pieces[0].shape[1], pieces[0].shape[2]
    depth = right_high.shape[0]
    y, xh, xl, z, core = place_of(lax.axis_index("row"), lax.axis_index("col"))
    column = xl * 8 + z
    for j, piece in enumerate(pieces):
        dy, c = j % 4, (core if j < 4 else 1 - core)
        for dxh in range(2):
            slot = ((y + dy) % 4 * 2 + (xh + dxh) % 2) * 2 + c
            start = share_ref[column * 16 + slot] * rows
            for part in range(0, rows, SEGMENT):
                place = pl.multiple_of(start + part, SEGMENT)
                block = column * (depth // BLK) + place // BLK
                for k in range(nsn):
                    flag = listed_ref[k, block].astype(jnp.float32)
                    high, low = split_value(piece[dxh * nsn + k, part : part + SEGMENT] * flag)
                    lanes = slice(k * width, (k + 1) * width)
                    right_high[pl.ds(place, SEGMENT), lanes] = high
                    right_low[pl.ds(place, SEGMENT), lanes] = low

    def dot(left, right):
        return jnp.dot(left, right, preferred_element_type=jnp.float32)

    for i in range(0, out.shape[0], BLK):
        band = slice(i, i + BLK)
        out[band, :] = (
            dot(left_high[band, :], right_high[...])
            + dot(left_high[band, :], right_low[...])
            + dot(left_low[band, :], right_high[...])
        )
    for x in range(2):
        opposite[x] = out[pl.ds(pl.multiple_of((x * 8 + (z + 4) % 8) * rows, SEGMENT), rows), :]


def multiply(listed, left_high, left_low, pieces):
    size, depth = left_high.shape
    rows = pieces[0].shape[1]
    wide = pieces[0].shape[0] // 2 * pieces[0].shape[2]
    whole = pl.BlockSpec(memory_space=pltpu.VMEM)
    scalars = pl.BlockSpec(memory_space=pltpu.SMEM)
    return pl.pallas_call(
        multiply_kernel,
        out_shape=[
            jax.ShapeDtypeStruct((size, wide), jnp.float32),
            jax.ShapeDtypeStruct((2, rows, wide), jnp.float32),
        ],
        in_specs=[scalars, scalars] + [whole] * (2 + len(pieces)),
        out_specs=[whole, whole],
        scratch_shapes=[pltpu.VMEM((depth, wide), jnp.bfloat16)] * 2,
        compiler_params=pltpu.CompilerParams(vmem_limit_bytes=VMEM_LIMIT),
        cost_estimate=pl.CostEstimate(flops=6 * size * wide * depth, bytes_accessed=12 * size * wide, transcendentals=0),
        name="multiply",
    )(jnp.asarray(np.array(SHARES, np.int32).reshape(-1)), listed, left_high, left_low, *pieces)


def terms_kernel(listed_ref, product, *refs):
    parts, (keep, give, left_high, left_low, right_high, right_low) = refs[:8], refs[8:]
    nsn, rows, width = parts[0].shape[0] // 2, parts[0].shape[1], parts[0].shape[2]
    row, col = lax.axis_index("row"), lax.axis_index("col")
    _, _, _, z, core = place_of(row, col)
    for d, part in enumerate(parts):
        chip = (z + d) % 8
        for x in range(2):
            here = slice((d * 2 + x) * rows, (d * 2 + x + 1) * rows)
            value = product[pl.ds(pl.multiple_of((x * 8 + chip) * rows, SEGMENT), rows), :]
            right_high[here, :], right_low[here, :] = split_value(value)
            first = (row * 32 + x * 16 + chip * 2 + core) * rows
            for s in range(0, rows, SEGMENT):
                for k in range(nsn):
                    flag = listed_ref[k, (first + s) // BLK].astype(jnp.float32)
                    high, low = split_value(part[x * nsn + k, s : s + SEGMENT] * flag)
                    spot = (slice(here.start + s, here.start + s + SEGMENT), slice(k * width, (k + 1) * width))
                    left_high[spot], left_low[spot] = high, low

    def dot(left, right, lanes):
        return lax.dot_general(
            left[:, lanes], right[:, lanes], (((0,), (0,)), ((), ())), preferred_element_type=jnp.float32
        )

    for k in range(nsn):
        lanes = slice(k * width, (k + 1) * width)
        value = (
            dot(left_high, right_high, lanes) + dot(left_high, right_low, lanes) + dot(left_low, right_high, lanes)
        )
        below, above = value[:, : width // 2], value[:, width // 2 :]
        keep[k] = jnp.where(core == 0, below, above)
        give[k] = jnp.where(core == 0, above, below)


def diagonal_terms(listed, product, parts):
    size, wide = product.shape
    nsn, width = parts[0].shape[0] // 2, parts[0].shape[2]
    whole = pl.BlockSpec(memory_space=pltpu.VMEM)
    return pl.pallas_call(
        terms_kernel,
        out_shape=[jax.ShapeDtypeStruct((nsn, width, width // 2), jnp.float32)] * 2,
        in_specs=[pl.BlockSpec(memory_space=pltpu.SMEM)] + [whole] * (1 + len(parts)),
        out_specs=[whole, whole],
        scratch_shapes=[pltpu.VMEM((size, wide), jnp.bfloat16)] * 4,
        compiler_params=pltpu.CompilerParams(vmem_limit_bytes=VMEM_LIMIT),
        cost_estimate=pl.CostEstimate(
            flops=6 * size * wide * width, bytes_accessed=8 * size * wide, transcendentals=0
        ),
        name="terms",
    )(listed, product, *parts)


def both(*arrays):
    return lax.optimization_barrier(arrays)


def per_device(inverse_block, factor_panel, diag_inverse, block_lists, list_counts):
    row, col = lax.axis_index("row"), lax.axis_index("col")
    y, xh, xl, z, core = place_of(row, col)
    nsn, rows, width = factor_panel.shape
    span = inverse_block.shape[1]

    def facing(array):
        return send(array, other_core)

    share = send(factor_panel, to_column)
    beside = send(factor_panel, other_xl)
    after, beside = both(core, beside)
    line = jnp.concatenate(
        [jnp.where(xl == 0, factor_panel, beside), jnp.where(xl == 0, beside, factor_panel)]
    )
    line_down, line_up = send(line, z_by(lambda c: 1)), send(line, z_by(lambda c: -1))
    halves = inverse_block.reshape(16, 2, rows, span)
    s_own = pick(halves, after, 1).reshape(16 * rows, span)
    s_other = facing(pick(halves, 1 - after, 1).reshape(16 * rows, span))
    share, line_down, line_up, s_other = both(share, line_down, line_up, s_other)

    near = send(share, other_xh)
    line_down2, line_up2 = send(line_down, z_by(lambda c: 1)), send(line_up, z_by(lambda c: -1))
    s_chip = jnp.concatenate(
        [jnp.where(core == 0, s_own, s_other), jnp.where(core == 0, s_other, s_own)], axis=1
    )
    s_high, s_low = split(s_chip)
    listed = listed_blocks(block_lists, list_counts, jnp.arange(block_lists.shape[1], dtype=jnp.int32))
    listed = listed.astype(jnp.int32)
    near, line_down2, line_up2, s_high, s_low, listed = both(near, line_down2, line_up2, s_high, s_low, listed)

    pair = jnp.concatenate([share, near])
    below, above = send(pair, y_by(lambda c: 1)), send(pair, y_by(lambda c: -1))
    line_down3, line_up3 = send(line_down2, z_by(lambda c: 1)), send(line_up2, z_by(lambda c: -1))
    pair_facing = facing(pair)
    below, above, line_down3, line_up3, pair_facing = both(below, above, line_down3, line_up3, pair_facing)

    far = send(jnp.where(core == 0, below, above), y_by(lambda c: 1 - 2 * c))
    line_far = send(jnp.where(core == 0, line_down3, line_up3), z_by(lambda c: 1 - 2 * c))
    below_facing, above_facing = facing(below), facing(above)
    far, line_far, below_facing, above_facing = both(far, line_far, below_facing, above_facing)
    pieces = [pair, above, far, below, pair_facing, above_facing, facing(far), below_facing]
    product, opposite = multiply(listed, s_high, s_low, pieces)
    stacked = product.reshape(2, 8, rows, nsn * width)

    def at(distance):
        return pick(stacked, (z + distance) % 8, 1)

    opposite = send(opposite, z_by(lambda c: 1 - 2 * c))
    keep, give = diagonal_terms(
        listed, product, [line, line_up, line_up2, line_up3, line_far, line_down3, line_down2, line_down]
    )
    terms = (keep + facing(give)).reshape(nsn, 2, 2, 2, width // 8, width // 2)
    terms = pick(terms, y % 2, 2) + send(pick(terms, 1 - y % 2, 2), y_pair)
    opposite, terms = both(opposite, terms)

    up = at(3) + jnp.where(core == 0, opposite, 0.0)
    down = at(-3) + jnp.where(core == 1, opposite, 0.0)
    up, down = send(up, z_by(lambda c: 1)), send(down, z_by(lambda c: -1))
    terms = pick(terms, y // 2, 1) + send(pick(terms, 1 - y // 2, 1), y_by(lambda c: 2))
    terms = pick(terms, xh, 1) + send(pick(terms, 1 - xh, 1), other_xh)
    up, down, terms = both(up, down, terms)

    up, down = send(at(2) + up, z_by(lambda c: 1)), send(at(-2) + down, z_by(lambda c: -1))
    terms = terms + send(terms, other_xl)
    terms = terms + send(terms, z_pair(1))
    up, down, terms = both(up, down, terms)

    up, down = send(at(1) + up, z_by(lambda c: 1)), send(at(-1) + down, z_by(lambda c: -1))
    terms = terms + send(terms, z_pair(2))
    up, down, terms = both(up, down, terms)

    partial = at(0) + up + down
    crossed = send(pick(partial, 1 - xl, 0), other_xl)
    total = pick(partial, xl, 0) + crossed
    row_blocks = ((row * 32 + col) * rows + jnp.arange(rows, dtype=jnp.int32)) // BLK
    mask = listed_blocks(block_lists, list_counts, row_blocks).astype(jnp.float32)
    solved = jnp.stack([total[:, k * width : (k + 1) * width] for k in range(nsn)])
    solved = -solved * mask[:, :, None]
    terms = terms + send(terms, z_pair(4))
    rest = facing(terms)
    diag_block = diag_inverse + jnp.concatenate(
        [jnp.where(core == 0, terms, rest), jnp.where(core == 0, rest, terms)], axis=2
    )
    return (solved, diag_block)


def solution(mesh):
    placed = (P("row", "col"), P(None, ("row", "col"), None), P(None, "row", None), P(), P())
    return jax.shard_map(
        per_device,
        mesh=mesh,
        in_specs=placed,
        out_specs=(P(None, ("row", "col"), None), P(None, "row", None)),
        check_vma=False,
    )
```

```python
import jax
import jax.numpy as jnp
import numpy as np
from jax import lax
from jax.experimental import pallas as pl
from jax.experimental.pallas import tpu as pltpu
from jax.sharding import PartitionSpec as P


BLK = 256
SEGMENT = 16
VMEM_LIMIT = 20 * 1024 * 1024
DIMS = (4, 2, 2, 8, 2)
AXES = ("row", "col")


def send(array, target):
    pairs = []
    for source in range(int(np.prod(DIMS))):
        place = tuple(int(i) for i in np.unravel_index(source, DIMS))
        pairs.append((source, int(np.ravel_multi_index(target(*place), DIMS))))
    return lax.ppermute(array, AXES, pairs)


def other_core(y, xh, xl, z, c):
    return (y, xh, xl, z, 1 - c)


def other_xl(y, xh, xl, z, c):
    return (y, xh, 1 - xl, z, c)


def other_xh(y, xh, xl, z, c):
    return (y, 1 - xh, xl, z, c)


def ahead(c):
    return 1 - 2 * c


def back(c):
    return 2 * c - 1


def y_by(move):
    return lambda y, xh, xl, z, c: ((y + move(c)) % 4, xh, xl, z, c)


def z_by(move):
    return lambda y, xh, xl, z, c: (y, xh, xl, (z + move(c)) % 8, c)


def y_pair(y, xh, xl, z, c):
    return (y ^ (3 if c else 1), xh, xl, z, c)


def z_pair(bit):
    return lambda y, xh, xl, z, c: (y, xh, xl, (((z + c) % 8 ^ bit) - c) % 8, c)


SHARES = (
    (5, 8, 10, 7, 14, 11, 4, 1, 2, 13, 15, 0, 9, 6, 3, 12),
    (11, 7, 4, 10, 0, 9, 3, 13, 5, 14, 1, 2, 12, 15, 6, 8),
    (1, 8, 11, 0, 7, 4, 12, 10, 6, 3, 9, 14, 2, 5, 15, 13),
    (12, 14, 7, 15, 11, 0, 8, 4, 2, 9, 3, 6, 13, 1, 5, 10),
    (8, 7, 13, 4, 11, 0, 14, 3, 10, 1, 12, 5, 2, 15, 6, 9),
    (1, 4, 14, 9, 3, 13, 2, 12, 5, 0, 8, 11, 6, 7, 15, 10),
    (15, 12, 1, 4, 3, 8, 6, 0, 9, 10, 13, 5, 11, 14, 2, 7),
    (9, 3, 13, 0, 15, 6, 2, 7, 12, 4, 5, 8, 1, 10, 11, 14),
    (14, 1, 12, 5, 2, 6, 13, 11, 8, 4, 9, 3, 15, 0, 10, 7),
    (12, 9, 3, 0, 10, 8, 1, 6, 14, 7, 4, 15, 11, 13, 5, 2),
    (5, 0, 3, 6, 14, 2, 1, 9, 13, 4, 10, 12, 11, 7, 8, 15),
    (8, 5, 13, 0, 2, 11, 7, 15, 12, 1, 4, 10, 3, 6, 14, 9),
    (6, 14, 15, 3, 7, 10, 12, 5, 8, 4, 2, 9, 0, 13, 1, 11),
    (1, 2, 9, 10, 4, 15, 11, 8, 7, 3, 14, 13, 12, 6, 5, 0),
    (9, 11, 3, 6, 13, 8, 10, 15, 2, 14, 7, 1, 0, 5, 4, 12),
    (3, 10, 7, 15, 0, 13, 4, 9, 14, 11, 1, 6, 8, 5, 2, 12),
)


def column_target():
    target = {}
    for column, shares in enumerate(SHARES):
        xl, z = column // 8, column % 8
        for slot, share in enumerate(shares):
            source = (xl * 2 + z // 4, z // 2 % 2, z % 2, share // 2, share % 2)
            target[source] = (slot // 4, slot // 2 % 2, xl, z, slot % 2)
    return target


COLUMN_TARGET = column_target()


def to_column(*place):
    return COLUMN_TARGET[place]


def listed_blocks(block_lists, list_counts, blocks):
    entries = jnp.arange(block_lists.shape[1], dtype=jnp.int32)
    active = entries[None, :] < list_counts[:, None]
    hits = (block_lists[:, None, :] == blocks[None, :, None]) & active[:, None, :]
    return jnp.any(hits, axis=2)


def pick(array, index, axis):
    return lax.dynamic_index_in_dim(array, index, axis, keepdims=False)


def place_of(row, col):
    return row // 2, row % 2, col // 16, col // 2 % 8, col % 2


def split(value):
    high = lax.reduce_precision(value, 8, 7)
    return high.astype(jnp.bfloat16), (value - high).astype(jnp.bfloat16)


def split_value(value):
    high = value.astype(jnp.bfloat16)
    return high, (value - high.astype(jnp.float32)).astype(jnp.bfloat16)


def multiply_kernel(share_ref, listed_ref, left_high, left_low, *refs):
    pieces, (out, opposite, right_high, right_low) = refs[:8], refs[8:]
    nsn, rows, width = pieces[0].shape[0] // 2, pieces[0].shape[1], pieces[0].shape[2]
    depth = right_high.shape[0]
    y, xh, xl, z, core = place_of(lax.axis_index("row"), lax.axis_index("col"))
    column = xl * 8 + z
    for j, piece in enumerate(pieces):
        dy, c = j % 4, (core if j < 4 else 1 - core)
        for dxh in range(2):
            slot = ((y + 4 + (1 - 2 * c) * dy) % 4 * 2 + (xh + dxh) % 2) * 2 + c
            start = share_ref[column * 16 + slot] * rows
            for part in range(0, rows, SEGMENT):
                place = pl.multiple_of(start + part, SEGMENT)
                block = column * (depth // BLK) + place // BLK
                for k in range(nsn):
                    flag = listed_ref[k, block].astype(jnp.float32)
                    high, low = split_value(piece[dxh * nsn + k, part : part + SEGMENT] * flag)
                    lanes = slice(k * width, (k + 1) * width)
                    right_high[pl.ds(place, SEGMENT), lanes] = high
                    right_low[pl.ds(place, SEGMENT), lanes] = low

    def dot(left, right):
        return jnp.dot(left, right, preferred_element_type=jnp.float32)

    for i in range(0, out.shape[0], BLK):
        band = slice(i, i + BLK)
        out[band, :] = (
            dot(left_high[band, :], right_high[...])
            + dot(left_high[band, :], right_low[...])
            + dot(left_low[band, :], right_high[...])
        )
    for x in range(2):
        opposite[x] = out[pl.ds(pl.multiple_of((x * 8 + (z + 4) % 8) * rows, SEGMENT), rows), :]


def multiply(listed, left_high, left_low, pieces):
    size, depth = left_high.shape
    rows = pieces[0].shape[1]
    wide = pieces[0].shape[0] // 2 * pieces[0].shape[2]
    whole = pl.BlockSpec(memory_space=pltpu.VMEM)
    scalars = pl.BlockSpec(memory_space=pltpu.SMEM)
    return pl.pallas_call(
        multiply_kernel,
        out_shape=[
            jax.ShapeDtypeStruct((size, wide), jnp.float32),
            jax.ShapeDtypeStruct((2, rows, wide), jnp.float32),
        ],
        in_specs=[scalars, scalars] + [whole] * (2 + len(pieces)),
        out_specs=[whole, whole],
        scratch_shapes=[pltpu.VMEM((depth, wide), jnp.bfloat16)] * 2,
        compiler_params=pltpu.CompilerParams(vmem_limit_bytes=VMEM_LIMIT),
        cost_estimate=pl.CostEstimate(flops=6 * size * wide * depth, bytes_accessed=12 * size * wide, transcendentals=0),
        name="multiply",
    )(jnp.asarray(np.array(SHARES, np.int32).reshape(-1)), listed, left_high, left_low, *pieces)


def terms_kernel(listed_ref, product, *refs):
    parts, (keep, give, left_high, left_low, right_high, right_low) = refs[:8], refs[8:]
    nsn, rows, width = parts[0].shape[0] // 2, parts[0].shape[1], parts[0].shape[2]
    row, col = lax.axis_index("row"), lax.axis_index("col")
    _, _, _, z, core = place_of(row, col)
    for d, part in enumerate(parts):
        chip = (z + 8 + (1 - 2 * core) * d) % 8
        for x in range(2):
            here = slice((d * 2 + x) * rows, (d * 2 + x + 1) * rows)
            value = product[pl.ds(pl.multiple_of((x * 8 + chip) * rows, SEGMENT), rows), :]
            right_high[here, :], right_low[here, :] = split_value(value)
            first = (row * 32 + x * 16 + chip * 2 + core) * rows
            for s in range(0, rows, SEGMENT):
                for k in range(nsn):
                    flag = listed_ref[k, (first + s) // BLK].astype(jnp.float32)
                    high, low = split_value(part[x * nsn + k, s : s + SEGMENT] * flag)
                    spot = (slice(here.start + s, here.start + s + SEGMENT), slice(k * width, (k + 1) * width))
                    left_high[spot], left_low[spot] = high, low

    def dot(left, right, lanes):
        return lax.dot_general(
            left[:, lanes], right[:, lanes], (((0,), (0,)), ((), ())), preferred_element_type=jnp.float32
        )

    for k in range(nsn):
        lanes = slice(k * width, (k + 1) * width)
        value = (
            dot(left_high, right_high, lanes) + dot(left_high, right_low, lanes) + dot(left_low, right_high, lanes)
        )
        below, above = value[:, : width // 2], value[:, width // 2 :]
        keep[k] = jnp.where(core == 0, below, above)
        give[k] = jnp.where(core == 0, above, below)


def diagonal_terms(listed, product, parts):
    size, wide = product.shape
    nsn, width = parts[0].shape[0] // 2, parts[0].shape[2]
    whole = pl.BlockSpec(memory_space=pltpu.VMEM)
    return pl.pallas_call(
        terms_kernel,
        out_shape=[jax.ShapeDtypeStruct((nsn, width, width // 2), jnp.float32)] * 2,
        in_specs=[pl.BlockSpec(memory_space=pltpu.SMEM)] + [whole] * (1 + len(parts)),
        out_specs=[whole, whole],
        scratch_shapes=[pltpu.VMEM((size, wide), jnp.bfloat16)] * 4,
        compiler_params=pltpu.CompilerParams(vmem_limit_bytes=VMEM_LIMIT),
        cost_estimate=pl.CostEstimate(
            flops=6 * size * wide * width, bytes_accessed=8 * size * wide, transcendentals=0
        ),
        name="terms",
    )(listed, product, *parts)


def both(*arrays):
    return lax.optimization_barrier(arrays)


def per_device(inverse_block, factor_panel, diag_inverse, block_lists, list_counts):
    row, col = lax.axis_index("row"), lax.axis_index("col")
    y, xh, xl, z, core = place_of(row, col)
    nsn, rows, width = factor_panel.shape
    span = inverse_block.shape[1]

    def facing(array):
        return send(array, other_core)

    share = send(factor_panel, to_column)
    beside = send(factor_panel, other_xl)
    after, beside = both(core, beside)
    halves = inverse_block.reshape(16, 2, rows, span)
    s_own = pick(halves, after, 1).reshape(16 * rows, span)
    s_other = facing(pick(halves, 1 - after, 1).reshape(16 * rows, span))
    share, beside, s_other = both(share, beside, s_other)

    near = send(share, other_xh)
    line = jnp.concatenate(
        [jnp.where(xl == 0, factor_panel, beside), jnp.where(xl == 0, beside, factor_panel)]
    )
    line_from1, line_to1 = send(line, z_by(ahead)), send(line, z_by(back))
    s_chip = jnp.concatenate(
        [jnp.where(core == 0, s_own, s_other), jnp.where(core == 0, s_other, s_own)], axis=1
    )
    s_high, s_low = split(s_chip)
    listed = listed_blocks(block_lists, list_counts, jnp.arange(block_lists.shape[1], dtype=jnp.int32))
    listed = listed.astype(jnp.int32)
    near, line_from1, line_to1, s_high, s_low, listed = both(near, line_from1, line_to1, s_high, s_low, listed)

    pair = jnp.concatenate([share, near])
    from1, to1 = send(pair, y_by(ahead)), send(pair, y_by(back))
    line_from2, line_to2 = send(line_from1, z_by(ahead)), send(line_to1, z_by(back))
    pair_facing = facing(pair)
    from1, to1, line_from2, line_to2, pair_facing = both(from1, to1, line_from2, line_to2, pair_facing)

    far = send(from1, y_by(ahead))
    line_from3, line_to3 = send(line_from2, z_by(ahead)), send(line_to2, z_by(back))
    from1_facing, to1_facing = facing(from1), facing(to1)
    far, line_from3, line_to3, from1_facing, to1_facing = both(far, line_from3, line_to3, from1_facing, to1_facing)
    line_far = send(line_from3, z_by(ahead))
    pieces = [pair, to1, far, from1, pair_facing, to1_facing, facing(far), from1_facing]
    product, opposite = multiply(listed, s_high, s_low, pieces)
    stacked = product.reshape(2, 8, rows, nsn * width)

    def at(distance):
        return pick(stacked, (z + (1 - 2 * core) * distance) % 8, 1)

    opposite = send(opposite, z_by(ahead))
    first, second = send(at(3) + opposite, z_by(ahead)), send(at(-3), z_by(back))
    first, second = send(at(2) + first, z_by(ahead)), send(at(-2) + second, z_by(back))
    first, second = send(at(1) + first, z_by(ahead)), send(at(-1) + second, z_by(back))
    partial = at(0) + first + second
    crossed = send(pick(partial, 1 - xl, 0), other_xl)
    total = pick(partial, xl, 0) + crossed
    row_blocks = ((row * 32 + col) * rows + jnp.arange(rows, dtype=jnp.int32)) // BLK
    mask = listed_blocks(block_lists, list_counts, row_blocks).astype(jnp.float32)
    solved = jnp.stack([total[:, k * width : (k + 1) * width] for k in range(nsn)])
    solved = -solved * mask[:, :, None]

    keep, give = diagonal_terms(
        listed, product, [line, line_to1, line_to2, line_to3, line_far, line_from3, line_from2, line_from1]
    )
    terms = (keep + facing(give)).reshape(nsn, 2, 2, 2, width // 8, width // 2)
    terms = pick(terms, y % 2, 2) + send(pick(terms, 1 - y % 2, 2), y_pair)
    terms = pick(terms, y // 2, 1) + send(pick(terms, 1 - y // 2, 1), y_by(lambda c: 2))
    terms = pick(terms, xh, 1) + send(pick(terms, 1 - xh, 1), other_xh)
    terms = terms + send(terms, other_xl)
    terms = terms + send(terms, z_pair(1))
    terms = terms + send(terms, z_pair(2))
    terms = terms + send(terms, z_pair(4))
    rest = facing(terms)
    diag_block = diag_inverse + jnp.concatenate(
        [jnp.where(core == 0, terms, rest), jnp.where(core == 0, rest, terms)], axis=2
    )
    return (solved, diag_block)


def solution(mesh):
    placed = (P("row", "col"), P(None, ("row", "col"), None), P(None, "row", None), P(), P())
    return jax.shard_map(
        per_device,
        mesh=mesh,
        in_specs=placed,
        out_specs=(P(None, ("row", "col"), None), P(None, "row", None)),
        check_vma=False,
    )
```

```python
import jax
import jax.numpy as jnp
import numpy as np
from jax import lax
from jax.experimental import pallas as pl
from jax.experimental.pallas import tpu as pltpu
from jax.sharding import PartitionSpec as P


BLK = 256
SEGMENT = 16
VMEM_LIMIT = 20 * 1024 * 1024
DIMS = (4, 2, 2, 8, 2)
AXES = ("row", "col")


def send(array, target):
    pairs = []
    for source in range(int(np.prod(DIMS))):
        place = tuple(int(i) for i in np.unravel_index(source, DIMS))
        pairs.append((source, int(np.ravel_multi_index(target(*place), DIMS))))
    return lax.ppermute(array, AXES, pairs)


def other_core(y, xh, xl, z, c):
    return (y, xh, xl, z, 1 - c)


def other_xl(y, xh, xl, z, c):
    return (y, xh, 1 - xl, z, c)


def other_xh(y, xh, xl, z, c):
    return (y, 1 - xh, xl, z, c)


def ahead(c):
    return 1 - 2 * c


def back(c):
    return 2 * c - 1


def y_by(move):
    return lambda y, xh, xl, z, c: ((y + move(c)) % 4, xh, xl, z, c)


def z_by(move):
    return lambda y, xh, xl, z, c: (y, xh, xl, (z + move(c)) % 8, c)


def z_pair(bit):
    return lambda y, xh, xl, z, c: (y, xh, xl, (((z + c) % 8 ^ bit) - c) % 8, c)


SHARES = (
    (5, 8, 10, 7, 14, 11, 4, 1, 2, 13, 15, 0, 9, 6, 3, 12),
    (11, 7, 4, 10, 0, 9, 3, 13, 5, 14, 1, 2, 12, 15, 6, 8),
    (1, 8, 11, 0, 7, 4, 12, 10, 6, 3, 9, 14, 2, 5, 15, 13),
    (12, 14, 7, 15, 11, 0, 8, 4, 2, 9, 3, 6, 13, 1, 5, 10),
    (8, 7, 13, 4, 11, 0, 14, 3, 10, 1, 12, 5, 2, 15, 6, 9),
    (1, 4, 14, 9, 3, 13, 2, 12, 5, 0, 8, 11, 6, 7, 15, 10),
    (15, 12, 1, 4, 3, 8, 6, 0, 9, 10, 13, 5, 11, 14, 2, 7),
    (9, 3, 13, 0, 15, 6, 2, 7, 12, 4, 5, 8, 1, 10, 11, 14),
    (14, 1, 12, 5, 2, 6, 13, 11, 8, 4, 9, 3, 15, 0, 10, 7),
    (12, 9, 3, 0, 10, 8, 1, 6, 14, 7, 4, 15, 11, 13, 5, 2),
    (5, 0, 3, 6, 14, 2, 1, 9, 13, 4, 10, 12, 11, 7, 8, 15),
    (8, 5, 13, 0, 2, 11, 7, 15, 12, 1, 4, 10, 3, 6, 14, 9),
    (6, 14, 15, 3, 7, 10, 12, 5, 8, 4, 2, 9, 0, 13, 1, 11),
    (1, 2, 9, 10, 4, 15, 11, 8, 7, 3, 14, 13, 12, 6, 5, 0),
    (9, 11, 3, 6, 13, 8, 10, 15, 2, 14, 7, 1, 0, 5, 4, 12),
    (3, 10, 7, 15, 0, 13, 4, 9, 14, 11, 1, 6, 8, 5, 2, 12),
)


def column_target():
    target = {}
    for column, shares in enumerate(SHARES):
        xl, z = column // 8, column % 8
        for slot, share in enumerate(shares):
            source = (xl * 2 + z // 4, z // 2 % 2, z % 2, share // 2, share % 2)
            target[source] = (slot // 4, slot // 2 % 2, xl, z, slot % 2)
    return target


COLUMN_TARGET = column_target()


def to_column(*place):
    return COLUMN_TARGET[place]


def listed_blocks(block_lists, list_counts, blocks):
    entries = jnp.arange(block_lists.shape[1], dtype=jnp.int32)
    active = entries[None, :] < list_counts[:, None]
    hits = (block_lists[:, None, :] == blocks[None, :, None]) & active[:, None, :]
    return jnp.any(hits, axis=2)


def pick(array, index, axis):
    return lax.dynamic_index_in_dim(array, index, axis, keepdims=False)


def place_of(row, col):
    return row // 2, row % 2, col // 16, col // 2 % 8, col % 2


def split(value):
    high = lax.reduce_precision(value, 8, 7)
    return high.astype(jnp.bfloat16), (value - high).astype(jnp.bfloat16)


def split_value(value):
    high = value.astype(jnp.bfloat16)
    return high, (value - high.astype(jnp.float32)).astype(jnp.bfloat16)


def multiply_kernel(share_ref, listed_ref, left_high, left_low, *refs):
    pieces, (out, opposite, right_high, right_low) = refs[:8], refs[8:]
    nsn, rows, width = pieces[0].shape[0] // 2, pieces[0].shape[1], pieces[0].shape[2]
    depth = right_high.shape[0]
    y, xh, xl, z, core = place_of(lax.axis_index("row"), lax.axis_index("col"))
    column = xl * 8 + z
    for j, piece in enumerate(pieces):
        dy, c = j % 4, (core if j < 4 else 1 - core)
        for dxh in range(2):
            slot = ((y + dy) % 4 * 2 + (xh + dxh) % 2) * 2 + c
            start = share_ref[column * 16 + slot] * rows
            for part in range(0, rows, SEGMENT):
                place = pl.multiple_of(start + part, SEGMENT)
                block = column * (depth // BLK) + place // BLK
                for k in range(nsn):
                    flag = listed_ref[k, block].astype(jnp.float32)
                    high, low = split_value(piece[dxh * nsn + k, part : part + SEGMENT] * flag)
                    lanes = slice(k * width, (k + 1) * width)
                    right_high[pl.ds(place, SEGMENT), lanes] = high
                    right_low[pl.ds(place, SEGMENT), lanes] = low

    def dot(left, right):
        return jnp.dot(left, right, preferred_element_type=jnp.float32)

    for i in range(0, out.shape[0], BLK):
        band = slice(i, i + BLK)
        out[band, :] = (
            dot(left_high[band, :], right_high[...])
            + dot(left_high[band, :], right_low[...])
            + dot(left_low[band, :], right_high[...])
        )
    for x in range(2):
        opposite[x] = out[pl.ds(pl.multiple_of((x * 8 + (z + 4) % 8) * rows, SEGMENT), rows), :]


def multiply(listed, left_high, left_low, pieces):
    size, depth = left_high.shape
    rows = pieces[0].shape[1]
    wide = pieces[0].shape[0] // 2 * pieces[0].shape[2]
    whole = pl.BlockSpec(memory_space=pltpu.VMEM)
    scalars = pl.BlockSpec(memory_space=pltpu.SMEM)
    return pl.pallas_call(
        multiply_kernel,
        out_shape=[
            jax.ShapeDtypeStruct((size, wide), jnp.float32),
            jax.ShapeDtypeStruct((2, rows, wide), jnp.float32),
        ],
        in_specs=[scalars, scalars] + [whole] * (2 + len(pieces)),
        out_specs=[whole, whole],
        scratch_shapes=[pltpu.VMEM((depth, wide), jnp.bfloat16)] * 2,
        compiler_params=pltpu.CompilerParams(vmem_limit_bytes=VMEM_LIMIT),
        cost_estimate=pl.CostEstimate(flops=6 * size * wide * depth, bytes_accessed=12 * size * wide, transcendentals=0),
        name="multiply",
    )(jnp.asarray(np.array(SHARES, np.int32).reshape(-1)), listed, left_high, left_low, *pieces)


def terms_kernel(listed_ref, product, *refs):
    parts, (keep, give, left_high, left_low, right_high, right_low) = refs[:8], refs[8:]
    nsn, rows, width = parts[0].shape[0] // 2, parts[0].shape[1], parts[0].shape[2]
    row, col = lax.axis_index("row"), lax.axis_index("col")
    _, _, _, z, core = place_of(row, col)
    for d, part in enumerate(parts):
        chip = (z + d) % 8
        for x in range(2):
            here = slice((d * 2 + x) * rows, (d * 2 + x + 1) * rows)
            value = product[pl.ds(pl.multiple_of((x * 8 + chip) * rows, SEGMENT), rows), :]
            right_high[here, :], right_low[here, :] = split_value(value)
            first = (row * 32 + x * 16 + chip * 2 + core) * rows
            for s in range(0, rows, SEGMENT):
                for k in range(nsn):
                    flag = listed_ref[k, (first + s) // BLK].astype(jnp.float32)
                    high, low = split_value(part[x * nsn + k, s : s + SEGMENT] * flag)
                    spot = (slice(here.start + s, here.start + s + SEGMENT), slice(k * width, (k + 1) * width))
                    left_high[spot], left_low[spot] = high, low

    def dot(left, right, lanes):
        return lax.dot_general(
            left[:, lanes], right[:, lanes], (((0,), (0,)), ((), ())), preferred_element_type=jnp.float32
        )

    for k in range(nsn):
        lanes = slice(k * width, (k + 1) * width)
        value = (
            dot(left_high, right_high, lanes) + dot(left_high, right_low, lanes) + dot(left_low, right_high, lanes)
        )
        below, above = value[:, : width // 2], value[:, width // 2 :]
        keep[k] = jnp.where(core == 0, below, above)
        give[k] = jnp.where(core == 0, above, below)


def diagonal_terms(listed, product, parts):
    size, wide = product.shape
    nsn, width = parts[0].shape[0] // 2, parts[0].shape[2]
    whole = pl.BlockSpec(memory_space=pltpu.VMEM)
    return pl.pallas_call(
        terms_kernel,
        out_shape=[jax.ShapeDtypeStruct((nsn, width, width // 2), jnp.float32)] * 2,
        in_specs=[pl.BlockSpec(memory_space=pltpu.SMEM)] + [whole] * (1 + len(parts)),
        out_specs=[whole, whole],
        scratch_shapes=[pltpu.VMEM((size, wide), jnp.bfloat16)] * 4,
        compiler_params=pltpu.CompilerParams(vmem_limit_bytes=VMEM_LIMIT),
        cost_estimate=pl.CostEstimate(
            flops=6 * size * wide * width, bytes_accessed=8 * size * wide, transcendentals=0
        ),
        name="terms",
    )(listed, product, *parts)


def both(*arrays):
    return lax.optimization_barrier(arrays)


def per_device(inverse_block, factor_panel, diag_inverse, block_lists, list_counts):
    row, col = lax.axis_index("row"), lax.axis_index("col")
    _, _, xl, z, core = place_of(row, col)
    nsn, rows, width = factor_panel.shape
    span = inverse_block.shape[1]

    def facing(array):
        return send(array, other_core)

    share = send(factor_panel, to_column)
    beside = send(factor_panel, other_xl)
    halves = inverse_block.reshape(16, 2, rows, span)
    s_own, s_give = pick(halves, core, 1), pick(halves, 1 - core, 1)
    s_own, s_other = s_own.reshape(16 * rows, span), facing(s_give.reshape(16 * rows, span))
    share, beside, s_other = both(share, beside, s_other)

    near = send(share, other_xh)
    line = jnp.concatenate(
        [jnp.where(xl == 0, factor_panel, beside), jnp.where(xl == 0, beside, factor_panel)]
    )
    line_down, line_up = send(line, z_by(lambda c: 1)), send(line, z_by(lambda c: -1))
    s_chip = jnp.concatenate(
        [jnp.where(core == 0, s_own, s_other), jnp.where(core == 0, s_other, s_own)], axis=1
    )
    s_high, s_low = split(s_chip)
    listed = listed_blocks(block_lists, list_counts, jnp.arange(block_lists.shape[1], dtype=jnp.int32))
    listed = listed.astype(jnp.int32)
    near, line_down, line_up, s_high, s_low, listed = both(near, line_down, line_up, s_high, s_low, listed)

    pair = jnp.concatenate([share, near])
    below, above = send(pair, y_by(lambda c: 1)), send(pair, y_by(lambda c: -1))
    line_down2, line_up2 = send(line_down, z_by(lambda c: 1)), send(line_up, z_by(lambda c: -1))
    pair_facing = facing(pair)
    below, above, line_down2, line_up2, pair_facing = both(below, above, line_down2, line_up2, pair_facing)

    far = send(jnp.where(core == 0, below, above), y_by(lambda c: 1 - 2 * c))
    line_down3, line_up3 = send(line_down2, z_by(lambda c: 1)), send(line_up2, z_by(lambda c: -1))
    below_facing, above_facing = facing(below), facing(above)
    far, line_down3, line_up3, below_facing, above_facing = both(
        far, line_down3, line_up3, below_facing, above_facing
    )
    line_far = send(jnp.where(core == 0, line_down3, line_up3), z_by(lambda c: 1 - 2 * c))
    pieces = [pair, above, far, below, pair_facing, above_facing, facing(far), below_facing]
    product, opposite = multiply(listed, s_high, s_low, pieces)
    stacked = product.reshape(2, 8, rows, nsn * width)

    def at(distance):
        return pick(stacked, (z + (1 - 2 * core) * distance) % 8, 1)

    opposite = send(opposite, z_by(ahead))
    first, second = send(at(3) + opposite, z_by(ahead)), send(at(-3), z_by(back))
    first, second = send(at(2) + first, z_by(ahead)), send(at(-2) + second, z_by(back))
    first, second = send(at(1) + first, z_by(ahead)), send(at(-1) + second, z_by(back))
    partial = at(0) + first + second
    crossed = send(pick(partial, 1 - xl, 0), other_xl)
    total = pick(partial, xl, 0) + crossed
    row_blocks = ((row * 32 + col) * rows + jnp.arange(rows, dtype=jnp.int32)) // BLK
    mask = listed_blocks(block_lists, list_counts, row_blocks).astype(jnp.float32)
    solved = jnp.stack([total[:, k * width : (k + 1) * width] for k in range(nsn)])
    solved = -solved * mask[:, :, None]

    keep, give = diagonal_terms(
        listed, product, [line, line_up, line_up2, line_up3, line_far, line_down3, line_down2, line_down]
    )
    terms = (keep + facing(give)).reshape(nsn, 8, width // 8, width // 2).transpose(1, 0, 2, 3)
    terms = lax.all_to_all(terms, "row", 0, 0, tiled=True)
    terms = jnp.sum(terms, axis=0)
    terms = terms + send(terms, other_xl)
    terms = terms + send(terms, z_pair(1))
    terms = terms + send(terms, z_pair(2))
    terms = terms + send(terms, z_pair(4))
    rest = facing(terms)
    diag_block = diag_inverse + jnp.concatenate(
        [jnp.where(core == 0, terms, rest), jnp.where(core == 0, rest, terms)], axis=2
    )
    return (solved, diag_block)


def solution(mesh):
    placed = (P("row", "col"), P(None, ("row", "col"), None), P(None, "row", None), P(), P())
    return jax.shard_map(
        per_device,
        mesh=mesh,
        in_specs=placed,
        out_specs=(P(None, ("row", "col"), None), P(None, "row", None)),
        check_vma=False,
    )
```

```python
import jax
import jax.numpy as jnp
import numpy as np
from jax import lax
from jax.experimental import pallas as pl
from jax.experimental.pallas import tpu as pltpu
from jax.sharding import PartitionSpec as P


BLK = 256
SEGMENT = 16
VMEM_LIMIT = 20 * 1024 * 1024
DIMS = (4, 2, 2, 8, 2)
AXES = ("row", "col")


def send(array, target):
    pairs = []
    for source in range(int(np.prod(DIMS))):
        place = tuple(int(i) for i in np.unravel_index(source, DIMS))
        pairs.append((source, int(np.ravel_multi_index(target(*place), DIMS))))
    return lax.ppermute(array, AXES, pairs)


def other_core(y, xh, xl, z, c):
    return (y, xh, xl, z, 1 - c)


def other_xl(y, xh, xl, z, c):
    return (y, xh, 1 - xl, z, c)


def other_xh(y, xh, xl, z, c):
    return (y, 1 - xh, xl, z, c)


def ahead(c):
    return 1 - 2 * c


def back(c):
    return 2 * c - 1


def y_by(move):
    return lambda y, xh, xl, z, c: ((y + move(c)) % 4, xh, xl, z, c)


def z_by(move):
    return lambda y, xh, xl, z, c: (y, xh, xl, (z + move(c)) % 8, c)


def z_pair(bit):
    return lambda y, xh, xl, z, c: (y, xh, xl, (((z + c) % 8 ^ bit) - c) % 8, c)


SHARES = (
    (5, 8, 10, 7, 14, 11, 4, 1, 2, 13, 15, 0, 9, 6, 3, 12),
    (11, 7, 4, 10, 0, 9, 3, 13, 5, 14, 1, 2, 12, 15, 6, 8),
    (1, 8, 11, 0, 7, 4, 12, 10, 6, 3, 9, 14, 2, 5, 15, 13),
    (12, 14, 7, 15, 11, 0, 8, 4, 2, 9, 3, 6, 13, 1, 5, 10),
    (8, 7, 13, 4, 11, 0, 14, 3, 10, 1, 12, 5, 2, 15, 6, 9),
    (1, 4, 14, 9, 3, 13, 2, 12, 5, 0, 8, 11, 6, 7, 15, 10),
    (15, 12, 1, 4, 3, 8, 6, 0, 9, 10, 13, 5, 11, 14, 2, 7),
    (9, 3, 13, 0, 15, 6, 2, 7, 12, 4, 5, 8, 1, 10, 11, 14),
    (14, 1, 12, 5, 2, 6, 13, 11, 8, 4, 9, 3, 15, 0, 10, 7),
    (12, 9, 3, 0, 10, 8, 1, 6, 14, 7, 4, 15, 11, 13, 5, 2),
    (5, 0, 3, 6, 14, 2, 1, 9, 13, 4, 10, 12, 11, 7, 8, 15),
    (8, 5, 13, 0, 2, 11, 7, 15, 12, 1, 4, 10, 3, 6, 14, 9),
    (6, 14, 15, 3, 7, 10, 12, 5, 8, 4, 2, 9, 0, 13, 1, 11),
    (1, 2, 9, 10, 4, 15, 11, 8, 7, 3, 14, 13, 12, 6, 5, 0),
    (9, 11, 3, 6, 13, 8, 10, 15, 2, 14, 7, 1, 0, 5, 4, 12),
    (3, 10, 7, 15, 0, 13, 4, 9, 14, 11, 1, 6, 8, 5, 2, 12),
)


def column_target():
    target = {}
    for column, shares in enumerate(SHARES):
        xl, z = column // 8, column % 8
        for slot, share in enumerate(shares):
            source = (xl * 2 + z // 4, z // 2 % 2, z % 2, share // 2, share % 2)
            target[source] = (slot // 4, slot // 2 % 2, xl, z, slot % 2)
    return target


COLUMN_TARGET = column_target()


def to_column(*place):
    return COLUMN_TARGET[place]


def listed_blocks(block_lists, list_counts, blocks):
    entries = jnp.arange(block_lists.shape[1], dtype=jnp.int32)
    active = entries[None, :] < list_counts[:, None]
    hits = (block_lists[:, None, :] == blocks[None, :, None]) & active[:, None, :]
    return jnp.any(hits, axis=2)


def pick(array, index, axis):
    return lax.dynamic_index_in_dim(array, index, axis, keepdims=False)


def place_of(row, col):
    return row // 2, row % 2, col // 16, col // 2 % 8, col % 2


def split(value):
    high = lax.reduce_precision(value, 8, 7)
    return high.astype(jnp.bfloat16), (value - high).astype(jnp.bfloat16)


def split_value(value):
    high = value.astype(jnp.bfloat16)
    return high, (value - high.astype(jnp.float32)).astype(jnp.bfloat16)


def multiply_kernel(share_ref, listed_ref, left_high, left_low, *refs):
    pieces, chunks, (out, right_high, right_low) = refs[:8], refs[8:16], refs[16:]
    nsn, rows, width = pieces[0].shape[0] // 2, pieces[0].shape[1], pieces[0].shape[2]
    depth = right_high.shape[0]
    y, xh, xl, z, core = place_of(lax.axis_index("row"), lax.axis_index("col"))
    column = xl * 8 + z
    for j, piece in enumerate(pieces):
        dy, c = j % 4, (core if j < 4 else 1 - core)
        for dxh in range(2):
            slot = ((y + dy) % 4 * 2 + (xh + dxh) % 2) * 2 + c
            start = share_ref[column * 16 + slot] * rows
            for part in range(0, rows, SEGMENT):
                place = pl.multiple_of(start + part, SEGMENT)
                block = column * (depth // BLK) + place // BLK
                for k in range(nsn):
                    flag = listed_ref[k, block].astype(jnp.float32)
                    high, low = split_value(piece[dxh * nsn + k, part : part + SEGMENT] * flag)
                    lanes = slice(k * width, (k + 1) * width)
                    right_high[pl.ds(place, SEGMENT), lanes] = high
                    right_low[pl.ds(place, SEGMENT), lanes] = low

    def dot(left, right):
        return jnp.dot(left, right, preferred_element_type=jnp.float32)

    for i in range(0, out.shape[0], BLK):
        band = slice(i, i + BLK)
        out[band, :] = (
            dot(left_high[band, :], right_high[...])
            + dot(left_high[band, :], right_low[...])
            + dot(left_low[band, :], right_high[...])
        )
    for j, chunk in enumerate(chunks):
        chip = (z + 8 + (1 - 2 * core) * j) % 8
        for x in range(2):
            chunk[x] = out[pl.ds(pl.multiple_of((x * 8 + chip) * rows, SEGMENT), rows), :]


def multiply(listed, left_high, left_low, pieces):
    size, depth = left_high.shape
    rows = pieces[0].shape[1]
    wide = pieces[0].shape[0] // 2 * pieces[0].shape[2]
    whole = pl.BlockSpec(memory_space=pltpu.VMEM)
    scalars = pl.BlockSpec(memory_space=pltpu.SMEM)
    return pl.pallas_call(
        multiply_kernel,
        out_shape=[jax.ShapeDtypeStruct((2, rows, wide), jnp.float32)] * 8,
        in_specs=[scalars, scalars] + [whole] * (2 + len(pieces)),
        out_specs=[whole] * 8,
        scratch_shapes=[pltpu.VMEM((size, wide), jnp.float32)] + [pltpu.VMEM((depth, wide), jnp.bfloat16)] * 2,
        compiler_params=pltpu.CompilerParams(vmem_limit_bytes=VMEM_LIMIT),
        cost_estimate=pl.CostEstimate(flops=6 * size * wide * depth, bytes_accessed=12 * size * wide, transcendentals=0),
        name="multiply",
    )(jnp.asarray(np.array(SHARES, np.int32).reshape(-1)), listed, left_high, left_low, *pieces)


def terms_kernel(listed_ref, *refs):
    chunks, parts, (keep, give, left_high, left_low, right_high, right_low) = refs[:8], refs[8:16], refs[16:]
    nsn, rows, width = parts[0].shape[0] // 2, parts[0].shape[1], parts[0].shape[2]
    row, col = lax.axis_index("row"), lax.axis_index("col")
    _, _, _, z, core = place_of(row, col)
    for d, part in enumerate(parts):
        chip = (z + d) % 8
        for x in range(2):
            here = slice((d * 2 + x) * rows, (d * 2 + x + 1) * rows)
            value = jnp.where(core == 0, chunks[d][x], chunks[-d % 8][x])
            right_high[here, :], right_low[here, :] = split_value(value)
            first = (row * 32 + x * 16 + chip * 2 + core) * rows
            for s in range(0, rows, SEGMENT):
                for k in range(nsn):
                    flag = listed_ref[k, (first + s) // BLK].astype(jnp.float32)
                    high, low = split_value(part[x * nsn + k, s : s + SEGMENT] * flag)
                    spot = (slice(here.start + s, here.start + s + SEGMENT), slice(k * width, (k + 1) * width))
                    left_high[spot], left_low[spot] = high, low

    def dot(left, right, lanes):
        return lax.dot_general(
            left[:, lanes], right[:, lanes], (((0,), (0,)), ((), ())), preferred_element_type=jnp.float32
        )

    for k in range(nsn):
        lanes = slice(k * width, (k + 1) * width)
        value = (
            dot(left_high, right_high, lanes) + dot(left_high, right_low, lanes) + dot(left_low, right_high, lanes)
        )
        below, above = value[:, : width // 2], value[:, width // 2 :]
        shape = keep.shape[:1] + keep.shape[2:]
        keep[:, k] = jnp.where(core == 0, below, above).reshape(shape)
        give[:, k] = jnp.where(core == 0, above, below).reshape(shape)


def diagonal_terms(listed, chunks, parts):
    nsn, width = parts[0].shape[0] // 2, parts[0].shape[2]
    size, wide = 8 * 2 * parts[0].shape[1], nsn * width
    whole = pl.BlockSpec(memory_space=pltpu.VMEM)
    return pl.pallas_call(
        terms_kernel,
        out_shape=[jax.ShapeDtypeStruct((8, nsn, width // 8, width // 2), jnp.float32)] * 2,
        in_specs=[pl.BlockSpec(memory_space=pltpu.SMEM)] + [whole] * (len(chunks) + len(parts)),
        out_specs=[whole, whole],
        scratch_shapes=[pltpu.VMEM((size, wide), jnp.bfloat16)] * 4,
        compiler_params=pltpu.CompilerParams(vmem_limit_bytes=VMEM_LIMIT),
        cost_estimate=pl.CostEstimate(
            flops=6 * size * wide * width, bytes_accessed=8 * size * wide, transcendentals=0
        ),
        name="terms",
    )(listed, *chunks, *parts)


def both(*arrays):
    return lax.optimization_barrier(arrays)


def per_device(inverse_block, factor_panel, diag_inverse, block_lists, list_counts):
    row, col = lax.axis_index("row"), lax.axis_index("col")
    _, _, xl, _, core = place_of(row, col)
    nsn, rows, width = factor_panel.shape
    span = inverse_block.shape[1]

    def facing(array):
        return send(array, other_core)

    share = send(factor_panel, to_column)
    beside = send(factor_panel, other_xl)
    halves = inverse_block.reshape(16, 2, rows, span)
    s_own, s_give = pick(halves, core, 1), pick(halves, 1 - core, 1)
    s_own, s_other = s_own.reshape(16 * rows, span), facing(s_give.reshape(16 * rows, span))
    share, beside, s_other = both(share, beside, s_other)

    near = send(share, other_xh)
    line = jnp.concatenate(
        [jnp.where(xl == 0, factor_panel, beside), jnp.where(xl == 0, beside, factor_panel)]
    )
    line_down, line_up = send(line, z_by(lambda c: 1)), send(line, z_by(lambda c: -1))
    s_chip = jnp.concatenate(
        [jnp.where(core == 0, s_own, s_other), jnp.where(core == 0, s_other, s_own)], axis=1
    )
    s_high, s_low = split(s_chip)
    listed = listed_blocks(block_lists, list_counts, jnp.arange(block_lists.shape[1], dtype=jnp.int32))
    listed = listed.astype(jnp.int32)
    near, line_down, line_up, s_high, s_low, listed = both(near, line_down, line_up, s_high, s_low, listed)

    pair = jnp.concatenate([share, near])
    below, above = send(pair, y_by(lambda c: 1)), send(pair, y_by(lambda c: -1))
    line_down2, line_up2 = send(line_down, z_by(lambda c: 1)), send(line_up, z_by(lambda c: -1))
    pair_facing = facing(pair)
    below, above, line_down2, line_up2, pair_facing = both(below, above, line_down2, line_up2, pair_facing)

    far = send(jnp.where(core == 0, below, above), y_by(lambda c: 1 - 2 * c))
    line_down3, line_up3 = send(line_down2, z_by(lambda c: 1)), send(line_up2, z_by(lambda c: -1))
    below_facing, above_facing = facing(below), facing(above)
    far, line_down3, line_up3, below_facing, above_facing = both(
        far, line_down3, line_up3, below_facing, above_facing
    )
    line_far = send(jnp.where(core == 0, line_down3, line_up3), z_by(lambda c: 1 - 2 * c))
    pieces = [pair, above, far, below, pair_facing, above_facing, facing(far), below_facing]
    chunks = multiply(listed, s_high, s_low, pieces)

    first = send(chunks[4], z_by(ahead))
    first, second = send(chunks[3] + first, z_by(ahead)), send(chunks[5], z_by(back))
    first, second = send(chunks[2] + first, z_by(ahead)), send(chunks[6] + second, z_by(back))
    first, second = send(chunks[1] + first, z_by(ahead)), send(chunks[7] + second, z_by(back))
    partial = chunks[0] + first + second
    crossed = send(pick(partial, 1 - xl, 0), other_xl)
    total = pick(partial, xl, 0) + crossed
    row_blocks = ((row * 32 + col) * rows + jnp.arange(rows, dtype=jnp.int32)) // BLK
    mask = listed_blocks(block_lists, list_counts, row_blocks).astype(jnp.float32)
    solved = jnp.stack([total[:, k * width : (k + 1) * width] for k in range(nsn)])
    solved = -solved * mask[:, :, None]

    keep, give = diagonal_terms(
        listed, chunks, [line, line_up, line_up2, line_up3, line_far, line_down3, line_down2, line_down]
    )
    terms = keep + facing(give)
    terms = lax.all_to_all(terms, "row", 0, 0, tiled=True)
    terms = jnp.sum(terms, axis=0)
    terms = terms + send(terms, other_xl)
    terms = terms + send(terms, z_pair(1))
    terms = terms + send(terms, z_pair(2))
    terms = terms + send(terms, z_pair(4))
    rest = facing(terms)
    diag_block = diag_inverse + jnp.concatenate(
        [jnp.where(core == 0, terms, rest), jnp.where(core == 0, rest, terms)], axis=2
    )
    return (solved, diag_block)


def solution(mesh):
    placed = (P("row", "col"), P(None, ("row", "col"), None), P(None, "row", None), P(), P())
    return jax.shard_map(
        per_device,
        mesh=mesh,
        in_specs=placed,
        out_specs=(P(None, ("row", "col"), None), P(None, "row", None)),
        check_vma=False,
    )
```

```python
import jax
import jax.numpy as jnp
import numpy as np
from jax import lax
from jax.experimental import pallas as pl
from jax.experimental.pallas import tpu as pltpu
from jax.sharding import PartitionSpec as P


BLK = 256
SEGMENT = 16
VMEM_LIMIT = 20 * 1024 * 1024
DIMS = (4, 2, 2, 8, 2)
AXES = ("row", "col")


def send(array, target):
    pairs = []
    for source in range(int(np.prod(DIMS))):
        place = tuple(int(i) for i in np.unravel_index(source, DIMS))
        pairs.append((source, int(np.ravel_multi_index(target(*place), DIMS))))
    return lax.ppermute(array, AXES, pairs)


def other_core(y, xh, xl, z, c):
    return (y, xh, xl, z, 1 - c)


def other_xl(y, xh, xl, z, c):
    return (y, xh, 1 - xl, z, c)


def other_xh(y, xh, xl, z, c):
    return (y, 1 - xh, xl, z, c)


def ahead(c):
    return 1 - 2 * c


def back(c):
    return 2 * c - 1


def y_by(move):
    return lambda y, xh, xl, z, c: ((y + move(c)) % 4, xh, xl, z, c)


def z_by(move):
    return lambda y, xh, xl, z, c: (y, xh, xl, (z + move(c)) % 8, c)


def z_pair(bit):
    return lambda y, xh, xl, z, c: (y, xh, xl, (((z + c) % 8 ^ bit) - c) % 8, c)


def other_xl_and_z_pair(y, xh, xl, z, c):
    return z_pair(1)(y, xh, 1 - xl, z, c)


SHARES = (
    (5, 8, 10, 7, 14, 11, 4, 1, 2, 13, 15, 0, 9, 6, 3, 12),
    (11, 7, 4, 10, 0, 9, 3, 13, 5, 14, 1, 2, 12, 15, 6, 8),
    (1, 8, 11, 0, 7, 4, 12, 10, 6, 3, 9, 14, 2, 5, 15, 13),
    (12, 14, 7, 15, 11, 0, 8, 4, 2, 9, 3, 6, 13, 1, 5, 10),
    (8, 7, 13, 4, 11, 0, 14, 3, 10, 1, 12, 5, 2, 15, 6, 9),
    (1, 4, 14, 9, 3, 13, 2, 12, 5, 0, 8, 11, 6, 7, 15, 10),
    (15, 12, 1, 4, 3, 8, 6, 0, 9, 10, 13, 5, 11, 14, 2, 7),
    (9, 3, 13, 0, 15, 6, 2, 7, 12, 4, 5, 8, 1, 10, 11, 14),
    (14, 1, 12, 5, 2, 6, 13, 11, 8, 4, 9, 3, 15, 0, 10, 7),
    (12, 9, 3, 0, 10, 8, 1, 6, 14, 7, 4, 15, 11, 13, 5, 2),
    (5, 0, 3, 6, 14, 2, 1, 9, 13, 4, 10, 12, 11, 7, 8, 15),
    (8, 5, 13, 0, 2, 11, 7, 15, 12, 1, 4, 10, 3, 6, 14, 9),
    (6, 14, 15, 3, 7, 10, 12, 5, 8, 4, 2, 9, 0, 13, 1, 11),
    (1, 2, 9, 10, 4, 15, 11, 8, 7, 3, 14, 13, 12, 6, 5, 0),
    (9, 11, 3, 6, 13, 8, 10, 15, 2, 14, 7, 1, 0, 5, 4, 12),
    (3, 10, 7, 15, 0, 13, 4, 9, 14, 11, 1, 6, 8, 5, 2, 12),
)


def column_target():
    target = {}
    for column, shares in enumerate(SHARES):
        xl, z = column // 8, column % 8
        for slot, share in enumerate(shares):
            source = (xl * 2 + z // 4, z // 2 % 2, z % 2, share // 2, share % 2)
            target[source] = (slot // 4, slot // 2 % 2, xl, z, slot % 2)
    return target


COLUMN_TARGET = column_target()


def to_column(*place):
    return COLUMN_TARGET[place]


def listed_blocks(block_lists, list_counts, blocks):
    entries = jnp.arange(block_lists.shape[1], dtype=jnp.int32)
    active = entries[None, :] < list_counts[:, None]
    hits = (block_lists[:, None, :] == blocks[None, :, None]) & active[:, None, :]
    return jnp.any(hits, axis=2)


def pick(array, index, axis):
    return lax.dynamic_index_in_dim(array, index, axis, keepdims=False)


def place_of(row, col):
    return row // 2, row % 2, col // 16, col // 2 % 8, col % 2


def split(value):
    high = lax.reduce_precision(value, 8, 7)
    return high.astype(jnp.bfloat16), (value - high).astype(jnp.bfloat16)


def split_value(value):
    high = value.astype(jnp.bfloat16)
    return high, (value - high.astype(jnp.float32)).astype(jnp.bfloat16)


def multiply_kernel(share_ref, listed_ref, left_high, left_low, *refs):
    pieces, chunks, (out, right_high, right_low) = refs[:8], refs[8:16], refs[16:]
    nsn, rows, width = pieces[0].shape[0] // 2, pieces[0].shape[1], pieces[0].shape[2]
    depth = right_high.shape[0]
    y, xh, xl, z, core = place_of(lax.axis_index("row"), lax.axis_index("col"))
    column = xl * 8 + z
    for j, piece in enumerate(pieces):
        dy, c = j % 4, (core if j < 4 else 1 - core)
        for dxh in range(2):
            slot = ((y + dy) % 4 * 2 + (xh + dxh) % 2) * 2 + c
            start = share_ref[column * 16 + slot] * rows
            for part in range(0, rows, SEGMENT):
                place = pl.multiple_of(start + part, SEGMENT)
                block = column * (depth // BLK) + place // BLK
                for k in range(nsn):
                    flag = listed_ref[k, block].astype(jnp.float32)
                    high, low = split_value(piece[dxh * nsn + k, part : part + SEGMENT] * flag)
                    lanes = slice(k * width, (k + 1) * width)
                    right_high[pl.ds(place, SEGMENT), lanes] = high
                    right_low[pl.ds(place, SEGMENT), lanes] = low

    def dot(left, right):
        return jnp.dot(left, right, preferred_element_type=jnp.float32)

    for i in range(0, out.shape[0], BLK):
        band = slice(i, i + BLK)
        out[band, :] = (
            dot(left_high[band, :], right_high[...])
            + dot(left_high[band, :], right_low[...])
            + dot(left_low[band, :], right_high[...])
        )
    for j, chunk in enumerate(chunks):
        chip = (z + 8 + (1 - 2 * core) * j) % 8
        for x in range(2):
            chunk[x] = out[pl.ds(pl.multiple_of((x * 8 + chip) * rows, SEGMENT), rows), :]


def multiply(listed, left_high, left_low, pieces):
    size, depth = left_high.shape
    rows = pieces[0].shape[1]
    wide = pieces[0].shape[0] // 2 * pieces[0].shape[2]
    whole = pl.BlockSpec(memory_space=pltpu.VMEM)
    scalars = pl.BlockSpec(memory_space=pltpu.SMEM)
    return pl.pallas_call(
        multiply_kernel,
        out_shape=[jax.ShapeDtypeStruct((2, rows, wide), jnp.float32)] * 8,
        in_specs=[scalars, scalars] + [whole] * (2 + len(pieces)),
        out_specs=[whole] * 8,
        scratch_shapes=[pltpu.VMEM((size, wide), jnp.float32)] + [pltpu.VMEM((depth, wide), jnp.bfloat16)] * 2,
        compiler_params=pltpu.CompilerParams(vmem_limit_bytes=VMEM_LIMIT),
        cost_estimate=pl.CostEstimate(flops=6 * size * wide * depth, bytes_accessed=12 * size * wide, transcendentals=0),
        name="multiply",
    )(jnp.asarray(np.array(SHARES, np.int32).reshape(-1)), listed, left_high, left_low, *pieces)


def terms_kernel(listed_ref, *refs):
    chunks, parts, (keep, give, left_high, left_low, right_high, right_low) = refs[:8], refs[8:16], refs[16:]
    nsn, rows, width = parts[0].shape[0] // 2, parts[0].shape[1], parts[0].shape[2]
    row, col = lax.axis_index("row"), lax.axis_index("col")
    _, _, _, z, core = place_of(row, col)
    for d, part in enumerate(parts):
        chip = (z + d) % 8
        for x in range(2):
            here = slice((d * 2 + x) * rows, (d * 2 + x + 1) * rows)
            value = jnp.where(core == 0, chunks[d][x], chunks[-d % 8][x])
            right_high[here, :], right_low[here, :] = split_value(value)
            first = (row * 32 + x * 16 + chip * 2 + core) * rows
            for s in range(0, rows, SEGMENT):
                for k in range(nsn):
                    flag = listed_ref[k, (first + s) // BLK].astype(jnp.float32)
                    high, low = split_value(part[x * nsn + k, s : s + SEGMENT] * flag)
                    spot = (slice(here.start + s, here.start + s + SEGMENT), slice(k * width, (k + 1) * width))
                    left_high[spot], left_low[spot] = high, low

    def dot(left, right, lanes):
        return lax.dot_general(
            left[:, lanes], right[:, lanes], (((0,), (0,)), ((), ())), preferred_element_type=jnp.float32
        )

    for k in range(nsn):
        lanes = slice(k * width, (k + 1) * width)
        value = (
            dot(left_high, right_high, lanes) + dot(left_high, right_low, lanes) + dot(left_low, right_high, lanes)
        )
        below, above = value[:, : width // 2], value[:, width // 2 :]
        shape = keep.shape[:1] + keep.shape[2:]
        keep[:, k] = jnp.where(core == 0, below, above).reshape(shape)
        give[:, k] = jnp.where(core == 0, above, below).reshape(shape)


def diagonal_terms(listed, chunks, parts):
    nsn, width = parts[0].shape[0] // 2, parts[0].shape[2]
    size, wide = 8 * 2 * parts[0].shape[1], nsn * width
    whole = pl.BlockSpec(memory_space=pltpu.VMEM)
    return pl.pallas_call(
        terms_kernel,
        out_shape=[jax.ShapeDtypeStruct((8, nsn, width // 8, width // 2), jnp.float32)] * 2,
        in_specs=[pl.BlockSpec(memory_space=pltpu.SMEM)] + [whole] * (len(chunks) + len(parts)),
        out_specs=[whole, whole],
        scratch_shapes=[pltpu.VMEM((size, wide), jnp.bfloat16)] * 4,
        compiler_params=pltpu.CompilerParams(vmem_limit_bytes=VMEM_LIMIT),
        cost_estimate=pl.CostEstimate(
            flops=6 * size * wide * width, bytes_accessed=8 * size * wide, transcendentals=0
        ),
        name="terms",
    )(listed, *chunks, *parts)


def both(*arrays):
    return lax.optimization_barrier(arrays)


def per_device(inverse_block, factor_panel, diag_inverse, block_lists, list_counts):
    row, col = lax.axis_index("row"), lax.axis_index("col")
    _, _, xl, _, core = place_of(row, col)
    nsn, rows, width = factor_panel.shape
    span = inverse_block.shape[1]

    def facing(array):
        return send(array, other_core)

    share = send(factor_panel, to_column)
    beside = send(factor_panel, other_xl)
    halves = inverse_block.reshape(16, 2, rows, span)
    s_own, s_give = pick(halves, core, 1), pick(halves, 1 - core, 1)
    s_own, s_other = s_own.reshape(16 * rows, span), facing(s_give.reshape(16 * rows, span))
    share, s_other = both(share, s_other)

    near = send(share, other_xh)
    line = jnp.concatenate(
        [jnp.where(xl == 0, factor_panel, beside), jnp.where(xl == 0, beside, factor_panel)]
    )
    line_down, line_up = send(line, z_by(lambda c: 1)), send(line, z_by(lambda c: -1))
    s_chip = jnp.concatenate(
        [jnp.where(core == 0, s_own, s_other), jnp.where(core == 0, s_other, s_own)], axis=1
    )
    s_high, s_low = split(s_chip)
    listed = listed_blocks(block_lists, list_counts, jnp.arange(block_lists.shape[1], dtype=jnp.int32))
    listed = listed.astype(jnp.int32)
    near, s_high, s_low, listed = both(near, s_high, s_low, listed)

    pair = jnp.concatenate([share, near])
    below, above = send(pair, y_by(lambda c: 1)), send(pair, y_by(lambda c: -1))
    line_down2, line_up2 = send(line_down, z_by(lambda c: 1)), send(line_up, z_by(lambda c: -1))
    pair_facing = facing(pair)
    far = send(jnp.where(core == 0, below, above), y_by(lambda c: 1 - 2 * c))
    line_down3, line_up3 = send(line_down2, z_by(lambda c: 1)), send(line_up2, z_by(lambda c: -1))
    below_facing, above_facing = facing(below), facing(above)
    far_facing = facing(far)
    line_far = send(jnp.where(core == 0, line_down3, line_up3), z_by(lambda c: 1 - 2 * c))
    pieces = [pair, above, far, below, pair_facing, above_facing, far_facing, below_facing]
    chunks = multiply(listed, s_high, s_low, pieces)

    first = send(chunks[4], z_by(ahead))
    first, second = send(chunks[3] + first, z_by(ahead)), send(chunks[5], z_by(back))
    first, second = send(chunks[2] + first, z_by(ahead)), send(chunks[6] + second, z_by(back))
    first, second = send(chunks[1] + first, z_by(ahead)), send(chunks[7] + second, z_by(back))
    partial = chunks[0] + first + second
    crossed = send(pick(partial, 1 - xl, 0), other_xl)
    total = pick(partial, xl, 0) + crossed
    row_blocks = ((row * 32 + col) * rows + jnp.arange(rows, dtype=jnp.int32)) // BLK
    mask = listed_blocks(block_lists, list_counts, row_blocks).astype(jnp.float32)
    solved = jnp.stack([total[:, k * width : (k + 1) * width] for k in range(nsn)])
    solved = -solved * mask[:, :, None]

    keep, give = diagonal_terms(
        listed, chunks, [line, line_up, line_up2, line_up3, line_far, line_down3, line_down2, line_down]
    )
    terms = keep + facing(give)
    terms = lax.all_to_all(terms, "row", 0, 0, tiled=True)
    terms = jnp.sum(terms, axis=0)
    there, across, past = send(terms, z_pair(1)), send(terms, other_xl), send(terms, other_xl_and_z_pair)
    terms = (terms + there) + (across + past)
    there, over, under = (send(terms, z_by(lambda c, k=k: k)) for k in (4, 2, -2))
    terms = (terms + there) + (over + under)
    rest = facing(terms)
    diag_block = diag_inverse + jnp.concatenate(
        [jnp.where(core == 0, terms, rest), jnp.where(core == 0, rest, terms)], axis=2
    )
    return (solved, diag_block)


def solution(mesh):
    placed = (P("row", "col"), P(None, ("row", "col"), None), P(None, "row", None), P(), P())
    return jax.shard_map(
        per_device,
        mesh=mesh,
        in_specs=placed,
        out_specs=(P(None, ("row", "col"), None), P(None, "row", None)),
        check_vma=False,
    )
```
